128 devices in a mesh: rollout: 4 (over x), context: 16 (over z, y), head: 2 (over core).
Axes of the slice: x: 4, y: 4, z: 4, core: 2. Of those that a mesh axis runs over, the one named last changes fastest.
Arguments:
- qkv: bfloat16 [3, 4, 2048, 32, 128], P(None, 'rollout', 'context', 'head'), may hold values from -18 to 18
- ssd_b: bfloat16 [4, 2048, 128], P('rollout', 'context'), may hold values from -5 to 5
- ssd_c: bfloat16 [4, 2048, 128], P('rollout', 'context'), may hold values from -0.5 to 0.5
- step_size: float32 [4, 2048, 64], P('rollout', 'context', 'head'), may hold values from 0 to 0.3, as said below
- decay_rate: float32 [64], P('head'), may hold values from 0.5 to 2
- value_weight: bfloat16 [4096], P('head'), may hold values from -0.09375 to 0.09375
- returns: float32 [4, 64], P('rollout'), may hold values from -4 to 4
- step_labels: int32 [4, 2048], P('rollout', 'context'), may hold values from 0 to 63, never falling along the last dimension, each value on 1 to 512 neighbouring positions
- lengths: int32 [4], replicated, may hold values from 512 to 2048, as said below
Outputs:
- loss: float32 [], replicated
- grad_qkv: bfloat16 [3, 4, 2048, 32, 128], P(None, 'rollout', 'context', 'head')
- grad_b: float32 [4, 2048, 128], P('rollout', 'context')
- grad_c: float32 [4, 2048, 128], P('rollout', 'context')
- grad_step: float32 [4, 2048, 64], P('rollout', 'context', 'head')
- grad_rate: float32 [64], P('head')
- grad_value: float32 [4096], P('head')
The draws below stay inside these ranges and needn't reach their ends.
Inputs may be any that keep to these rules, and one draw needn't show every extreme that they name: `step_size`: positive. `lengths`: one rollout in every draw is full. `step_labels`: never falling along a rollout.
All inputs are finite; a program needn't handle non-finite values.
Results may differ from the reference program's by a relative error of at most 0.011.
Values may be sent and summed in bfloat16 or wider, within the bound.
A program may use at most 192 MiB of HBM per device.

```python
import math
import jax
import jax.numpy as jnp
import numpy as np
from jax import lax

TOK_DEV = 128
HA = 32
HD = 128
MH = 64
MP = 64
NS = 128
NSTEPS = 64
ROLLOUT_COUNT = 4
ROLLOUT_LENGTH = 2048
STEP_MOST = 512


def draw_qkv(key, part):
    full_shape = (3, ROLLOUT_COUNT, ROLLOUT_LENGTH, HA, HD)
    base_draw = jnp.clip(jax.random.normal(key, full_shape, jnp.float32), -5.0, 5.0)
    return base_draw.astype(jnp.bfloat16)


def draw_step_size(key, part):
    quick_random_key, rate_random_key, jagged_random_key, spike_random_key = jax.random.split(key, 4)
    fast_share = 0.5
    fast_heads = jax.random.uniform(quick_random_key, (MH,), jnp.float32) < fast_share
    level = jax.random.uniform(rate_random_key, (MH,), jnp.float32)
    fast_rate = 1.0 / 50.0 * (50.0 / 30.0) ** level
    slow_rate = 0.05 / ROLLOUT_LENGTH * 6.0 ** level
    head_rate = jnp.where(fast_heads, fast_rate, slow_rate)
    roughness = jax.random.uniform(jagged_random_key, (ROLLOUT_COUNT, ROLLOUT_LENGTH, MH), jnp.float32, 0.5, 1.5)
    per_step_values = head_rate[None, None, :] * roughness
    spike_position = jax.random.randint(spike_random_key, (ROLLOUT_COUNT, 2), 0, ROLLOUT_LENGTH)
    spike_landed = jnp.any(jnp.arange(ROLLOUT_LENGTH)[None, :, None] == spike_position[:, None, :], axis=2)
    return jnp.where(spike_landed[:, :, None], 0.3, per_step_values).astype(jnp.float32)


def draw_lengths(key, part):
    key_len, key_full = jax.random.split(key)
    drawn = jax.random.randint(key_len, (ROLLOUT_COUNT,), ROLLOUT_LENGTH // 4, ROLLOUT_LENGTH + 1)
    chosen = jax.random.randint(key_full, (), 0, ROLLOUT_COUNT)
    return jnp.where(jnp.arange(ROLLOUT_COUNT) == chosen, ROLLOUT_LENGTH, drawn).astype(jnp.int32)


def block_levels(rng, extent, cuts, smallest, high):
    level, own = 1.0, jax.random.fold_in(rng, 6)
    for dim, parts in cuts:
        draws = jnp.exp(jax.random.uniform(jax.random.fold_in(own, dim), (parts,), jnp.float32, smallest / len(cuts), high / len(cuts)))
        level = level * jnp.repeat(draws, extent[dim] // parts).reshape([-1 if axis == dim else 1 for axis in range(len(extent))])
    return level


def length_profile(count, total, most, lean):
    loads = [(1 << 20) // math.isqrt(rank ** lean) + 1 for rank in range(2, count + 1)]
    surplus, given = total - most - (count - 1), [1] * (count - 1)
    while surplus > 0:
        candidates = [i for i in range(count - 1) if given[i] < most]
        mass, budget = sum([loads[i] for i in candidates]), surplus
        for i in candidates:
            addition = min(most - given[i], max(1, budget * loads[i] // mass), surplus)
            given[i] = given[i] + addition
            surplus = surplus - addition
    return np.array([most] + given)


def uneven_parts(rng, count, total, limit, skew):
    if count == 2:
        one = jax.random.randint(rng, (), max(1, total - limit), min(limit, total - 1) + 1)
        return jnp.stack([one, total - one])
    sizes = jnp.asarray(length_profile(count, total, limit, skew), jnp.int32)
    couples = (count - 1) // 2
    donor, receiver = sizes[1:1 + 2 * couples:2], sizes[2:2 + 2 * couples:2]
    slack = jnp.minimum(donor - 1, limit - receiver)
    moved = jax.random.randint(jax.random.fold_in(rng, 1), (couples,), 0, 1 << 20) % (slack + 1)
    sizes = sizes.at[1:1 + 2 * couples:2].set(donor - moved).at[2:2 + 2 * couples:2].set(receiver + moved)
    return sizes[jax.random.permutation(jax.random.fold_in(rng, 2), count)]


def bell_draw(own_key, shape, scale, reach, cuts=(), kind=jnp.bfloat16):
    loudness = block_levels(own_key, shape, cuts, -0.22, 0.18) if cuts else 1.0
    values = jax.random.normal(own_key, shape, jnp.float32) * scale * loudness
    return jnp.minimum(jnp.maximum(values, -reach), reach).astype(kind)


def setup_inputs(seed: int = 0) -> dict:
    keys = jax.random.split(jax.random.key(seed), 10)
    qkv = draw_qkv(jax.random.fold_in(keys[9], 71), 0)
    ssd_b = bell_draw(keys[1], (ROLLOUT_COUNT, ROLLOUT_LENGTH, NS), 1.0, 5.0, ((0, 4), (1, 16)))
    ssd_c = bell_draw(keys[2], (ROLLOUT_COUNT, ROLLOUT_LENGTH, NS), NS ** -0.5, 0.5, ((0, 4), (1, 16)))
    step_size = draw_step_size(jax.random.fold_in(keys[9], 71), 0)
    decay_rate = jnp.clip(jnp.exp(math.log(2.0) - 1.3862944 * jax.random.uniform(keys[4], (MH,), jnp.float32) ** block_levels(keys[4], (MH,), ((0, 2),), -0.2, 0.2)), 0.5, 2.0)
    value_weight = bell_draw(keys[5], (MH * MP,), (MH * MP) ** -0.5, 0.09375, ((0, 2),))
    returns = bell_draw(keys[6], (ROLLOUT_COUNT, NSTEPS), 1.0, 4.0, ((0, 4),), jnp.float32)
    step_labels = jax.vmap(lambda own: jnp.searchsorted(jnp.cumsum(uneven_parts(own, NSTEPS, ROLLOUT_LENGTH, STEP_MOST, 2)), jnp.arange(ROLLOUT_LENGTH), side="right"))(jax.random.split(keys[7], ROLLOUT_COUNT)).reshape((ROLLOUT_COUNT, ROLLOUT_LENGTH)).astype(jnp.int32)
    lengths = draw_lengths(jax.random.fold_in(keys[9], 71), 0)
    return dict(qkv=qkv, ssd_b=ssd_b, ssd_c=ssd_c, step_size=step_size, decay_rate=decay_rate, value_weight=value_weight, returns=returns, step_labels=step_labels, lengths=lengths)


MASK_FILL = -1e+30
NORM_EPS = 1e-05
HIGHEST_PREC = lax.Precision.HIGHEST

def block_probs(query_block, key_rows, first_row):
    head_size = query_block.shape[1]
    scores = lax.dot_general(query_block, key_rows, (((1,), (1,)), ((), ())), preferred_element_type=jnp.float32)
    scores = scores * (1.0 / math.sqrt(head_size))
    row_ids = first_row + jnp.arange(query_block.shape[0], dtype=jnp.int32)[:, None]
    col_ids = jnp.arange(key_rows.shape[0], dtype=jnp.int32)[None, :]
    scores = jnp.where(col_ids <= row_ids, scores, MASK_FILL)
    row_max = lax.stop_gradient(lax.optimization_barrier(jnp.max(scores, axis=1, keepdims=True)))
    weights = jnp.exp(scores - row_max)
    return weights / lax.optimization_barrier(jnp.sum(weights, axis=1, keepdims=True))

def head_forward(queries, key_rows, values, offset):
    block_rows = min(512, queries.shape[0])
    block_count = queries.shape[0] // block_rows
    blocks = queries.reshape(block_count, block_rows, queries.shape[1])
    starts = offset + jnp.arange(block_count, dtype=jnp.int32) * block_rows

    def one_block(operands):
        probability = block_probs(operands[0], key_rows, operands[1]).astype(jnp.bfloat16)
        return jnp.dot(probability, values, preferred_element_type=jnp.float32).astype(jnp.bfloat16)
    return lax.map(one_block, (blocks, starts)).reshape(queries.shape)

def head_backward(queries, key_rows, values, grad_out, offset):
    head_size = queries.shape[1]
    block_rows = min(512, queries.shape[0])
    block_count = queries.shape[0] // block_rows
    blocks = queries.reshape(block_count, block_rows, head_size)
    grad_blocks = grad_out.reshape(block_count, block_rows, head_size)
    starts = offset + jnp.arange(block_count, dtype=jnp.int32) * block_rows

    def one_block(carried, operands):
        key_grad, value_grad = carried
        query_block, grad_block, first_row = operands
        probability = block_probs(query_block, key_rows, first_row)
        rounded = probability.astype(jnp.bfloat16)
        value_grad = value_grad + lax.dot_general(rounded, grad_block, (((0,), (0,)), ((), ())), preferred_element_type=jnp.float32)
        prob_grad = lax.dot_general(grad_block, values, (((1,), (1,)), ((), ())), preferred_element_type=jnp.float32)
        centre = lax.optimization_barrier(jnp.sum(probability * prob_grad, axis=1, keepdims=True))
        score_grad = (probability * (prob_grad - centre) * (1.0 / math.sqrt(head_size))).astype(jnp.bfloat16)
        query_grad = jnp.dot(score_grad, key_rows, preferred_element_type=jnp.float32).astype(jnp.bfloat16)
        key_grad = key_grad + lax.dot_general(score_grad, query_block, (((0,), (0,)), ((), ())), preferred_element_type=jnp.float32)
        return ((key_grad, value_grad), query_grad)
    zero_grad = jnp.zeros(key_rows.shape, jnp.float32)
    totals, query_grad = lax.scan(one_block, (zero_grad, zero_grad), (blocks, grad_blocks, starts))
    return (query_grad.reshape(queries.shape), totals[0], totals[1])

def attend(queries, key_rows, values, offset):

    def per_head(operands):
        return head_forward(operands[0], operands[1], operands[2], offset)
    result = lax.map(per_head, (jnp.swapaxes(queries, 0, 1), jnp.swapaxes(key_rows, 0, 1), jnp.swapaxes(values, 0, 1)))
    return jnp.swapaxes(result, 0, 1)

def attend_back(queries, key_rows, values, grad_out, offset):

    def per_head(operands):
        return head_backward(operands[0], operands[1], operands[2], operands[3], offset)
    query_grad, key_grad, value_grad = lax.map(per_head, (jnp.swapaxes(queries, 0, 1), jnp.swapaxes(key_rows, 0, 1), jnp.swapaxes(values, 0, 1), jnp.swapaxes(grad_out, 0, 1)))
    return (jnp.swapaxes(query_grad, 0, 1), jnp.swapaxes(key_grad, 0, 1), jnp.swapaxes(value_grad, 0, 1))

def ssd_parts(inputs, step_dt, rate, b_proj):
    cumulative = jnp.cumsum(-step_dt * rate[None, :], axis=0)
    tail_decay = jnp.exp(cumulative[-1:, :] - cumulative)
    state_term = jnp.einsum('th,thp,tn->hpn', tail_decay, inputs, b_proj, precision=HIGHEST_PREC)
    return (jnp.exp(cumulative[-1]), state_term)

def ssd_output(inputs, step_dt, rate, b_proj, c_proj, state_in):
    cumulative = jnp.cumsum(-step_dt * rate[None, :], axis=0)
    cum_heads = cumulative.T
    row_count = inputs.shape[0]
    causal = (jnp.arange(row_count)[:, None] >= jnp.arange(row_count)[None, :])[None]
    log_gap = jnp.where(causal, cum_heads[:, :, None] - cum_heads[:, None, :], 0.0)
    decay_mask = jnp.where(causal, jnp.exp(log_gap), 0.0)
    inner_prod = lax.optimization_barrier(jnp.sum(c_proj[:, None, :] * b_proj[None, :, :], axis=2))
    local_out = jnp.einsum('hts,shp->thp', decay_mask * inner_prod[None], inputs, precision=HIGHEST_PREC)
    carried = jnp.einsum('tn,hpn->thp', c_proj, state_in, precision=HIGHEST_PREC) * jnp.exp(cumulative)[:, :, None]
    return local_out + carried

def value_part(outputs, weight):
    norm_scale = lax.rsqrt(lax.optimization_barrier(jnp.mean(outputs * outputs, axis=2, keepdims=True)) + NORM_EPS)
    normed = (outputs * norm_scale).reshape(outputs.shape[0], -1)
    return jnp.dot(normed, weight, precision=HIGHEST_PREC)

def whole_ssd(inputs, step_dt, rate, b_proj, c_proj):
    pieces = inputs.shape[0] // TOK_DEV

    def split_rows(array):
        return array.reshape((pieces, TOK_DEV) + array.shape[1:])

    def advance(state_in, operands):
        part_in, part_step, part_b, part_c = operands
        outputs = ssd_output(part_in, part_step, rate, part_b, part_c, state_in)
        decays, state_term = ssd_parts(part_in, part_step, rate, part_b)
        return (decays[:, None, None] * state_in + state_term, outputs)
    zero_state = jnp.zeros((inputs.shape[1], inputs.shape[2], b_proj.shape[1]), jnp.float32)
    final_state, outputs = lax.scan(advance, zero_state, (split_rows(inputs), split_rows(step_dt), split_rows(b_proj), split_rows(c_proj)))
    return outputs.reshape(inputs.shape)

def post_attention(attended, step_dt, rate, b_proj, c_proj, weight):
    inputs = attended.reshape(attended.shape[0], MH, MP).astype(jnp.float32)
    return value_part(whole_ssd(inputs, step_dt, rate, b_proj, c_proj), weight)

def reference(qkv, ssd_b, ssd_c, step_size, decay_rate, value_weight, returns, step_labels, lengths):
    weight_full = value_weight.astype(jnp.float32)

    def per_rollout(operands):
        qkv_one, b_one, c_one, step_one, table_one, labels_one, length_one = operands
        zero_offset = jnp.int32(0)
        attended = attend(qkv_one[0], qkv_one[1], qkv_one[2], zero_offset)
        b_rows = b_one.astype(jnp.float32)
        c_rows = c_one.astype(jnp.float32)
        value, post_back = jax.vjp(post_attention, attended, step_one, decay_rate, b_rows, c_rows, weight_full)
        onehot = (labels_one[:, None] == jnp.arange(NSTEPS, dtype=jnp.int32)[None, :]).astype(jnp.float32)
        target = jnp.dot(onehot, table_one, precision=HIGHEST_PREC)
        valid_mask = (jnp.arange(value.shape[0], dtype=jnp.int32) < length_one).astype(jnp.float32)
        error_term = (value - target) * valid_mask
        loss_one = 0.5 * jnp.sum(error_term * error_term)
        attended_grad, step_grad, rate_grad, b_grad, c_grad, weight_grad = post_back(error_term)
        query_grad, key_grad, value_grad = attend_back(qkv_one[0], qkv_one[1], qkv_one[2], attended_grad, zero_offset)
        qkv_grad = jnp.stack([query_grad, key_grad.astype(jnp.bfloat16), value_grad.astype(jnp.bfloat16)])
        return (loss_one, qkv_grad, b_grad, c_grad, step_grad, rate_grad, weight_grad)
    losses, qkv_grads, b_grads, c_grads, step_grads, rate_grads, weight_grads = lax.map(per_rollout, (jnp.swapaxes(qkv, 0, 1), ssd_b, ssd_c, step_size, returns, step_labels, lengths))
    loss = jnp.sum(losses) / jnp.sum(lengths).astype(jnp.float32)
    return (loss, jnp.swapaxes(qkv_grads, 0, 1), b_grads, c_grads, step_grads, lax.optimization_barrier(jnp.sum(rate_grads, axis=0)), lax.optimization_barrier(jnp.sum(weight_grads, axis=0)))
```

```python
import functools
import math

import jax
import jax.numpy as jnp
from jax import lax
from jax.experimental import pallas as pl
from jax.experimental.pallas import tpu as pltpu
from jax.sharding import PartitionSpec as P

NORM_EPS = 1e-05
HI = lax.Precision.HIGHEST
F32 = jnp.float32
BF16 = jnp.bfloat16
T = 2048
W = 256
NB = T // W
D = 128
SCALE = 1.0 / math.sqrt(128.0)
LOG2E = 1.4426950408889634


def dot_nn(a, b, precision=None):
    return lax.dot_general(a, b, (((1,), (0,)), ((), ())), precision=precision, preferred_element_type=F32)


def dot_nt(a, b, precision=None):
    return lax.dot_general(a, b, (((1,), (1,)), ((), ())), precision=precision, preferred_element_type=F32)


def dot_tn(a, b, precision=None):
    return lax.dot_general(a, b, (((0,), (0,)), ((), ())), precision=precision, preferred_element_type=F32)


def parts(a):
    high = a.astype(BF16)
    return high, (a - high.astype(F32)).astype(BF16)


def rows(i):
    return pl.ds(i * W, W)


def iota(shape, dim):
    return lax.broadcasted_iota(jnp.int32, shape, dim)


def head_select():
    return jnp.where(iota((8, D), 1) // 64 == iota((8, D), 0), 1.0, 0.0).astype(F32)


def head_mean():
    return jnp.where(iota((D, D), 0) // 64 == iota((D, D), 1) // 64, 1.0 / 64.0, 0.0).astype(F32)


def attention_forward(q, k, v, p, x):
    causal = iota((W, W), 0) >= iota((W, W), 1)
    c = SCALE * LOG2E
    for i in range(NB):
        qi = q[rows(i), :]
        diag = jnp.where(causal, dot_nt(qi, k[rows(i), :]) * c, -1e30)
        top = jnp.max(diag, axis=1, keepdims=True)
        if i:
            past = dot_nt(qi, k[: i * W, :]) * c
            top = jnp.maximum(top, jnp.max(past, axis=1, keepdims=True))
            past = jnp.exp2(past - top)
        diag = jnp.exp2(diag - top)
        total = jnp.sum(diag, axis=1, keepdims=True)
        if i:
            total = total + jnp.sum(past, axis=1, keepdims=True)
        inverse = 1.0 / total
        pd = (diag * inverse).astype(BF16)
        p[rows(i), rows(i)] = pd
        o = dot_nn(pd, v[rows(i), :])
        if i:
            pp = (past * inverse).astype(BF16)
            p[rows(i), : i * W] = pp
            o = o + dot_nn(pp, v[: i * W, :])
        x[rows(i), :] = o.astype(BF16)


def ssd_forward(x, b, c, step, rate, weight, cum_rows, cum_cols, state, mask, gmask, unit, normed, carried, value):
    hsel = head_select()
    hmean = head_mean()
    upto = jnp.where(iota((W, W), 0) <= iota((W, W), 1), 1.0, 0.0).astype(F32)
    causal = iota((W, W), 0) >= iota((W, W), 1)
    first = iota((W, D), 1) < 64
    w8 = weight[...]
    w1 = w8[0:1, :]
    st = jnp.zeros((D, D), F32)
    for i in range(NB):
        la = -(step[:, rows(i)] * rate[:, 0:1])
        cr = dot_nn(la, upto, HI)
        ce = dot_tn(cr, hsel, HI)
        cum_rows[:, rows(i)] = cr
        cum_cols[rows(i), :] = ce
        end = ce[W - 1 : W, :]
        bi, ci, xi = b[rows(i), :], c[rows(i), :], x[rows(i), :]
        g = dot_nt(ci, bi)
        y = None
        for h in range(2):
            gap = ce[:, 64 * h : 64 * h + 1] - cr[h : h + 1, :]
            m = jnp.exp(jnp.where(causal, gap, -1e30))
            gm = (g * m).astype(BF16)
            mask[h, rows(i), :] = m.astype(BF16)
            gmask[h, rows(i), :] = gm
            xh = jnp.where(first == (h == 0), xi, jnp.zeros_like(xi))
            gl = (g * m - gm.astype(F32)).astype(BF16)
            part = dot_nn(gm, xh) + dot_nn(gl, xh)
            y = part if y is None else y + part
        state[i] = st
        ca = jnp.exp(ce) * (dot_nn(ci, parts(st)[0]) + dot_nn(ci, parts(st)[1]))
        carried[rows(i), :] = ca
        y = y + ca
        xh, xl = parts(xi.astype(F32) * jnp.exp(end - ce))
        st = jnp.exp(end) * st + (dot_tn(bi, xh) + dot_tn(bi, xl))
        r = lax.rsqrt(dot_nn(y * y, hmean, HI) + NORM_EPS)
        n = y * r
        a = dot_nn(n * w1, hmean, HI)
        unit[rows(i), :] = r * (w1 - n * a)
        normed[rows(i), :] = n
        value[:, rows(i)] = dot_nt(w8, n, HI)


def ssd_backward(err, x, b, c, step, rate, cum_rows, cum_cols, state, mask, gmask, unit, normed, carried,
                 dx, db, dc, gstep, grate, gvalue):
    hsel = head_select()
    row0 = jnp.where(iota((8, D), 0) == 0, 1.0, 0.0).astype(F32)
    suffix = jnp.where(iota((W, W), 0) >= iota((W, W), 1), 1.0, 0.0).astype(F32)
    prefix = jnp.where(iota((W, W), 0) < iota((W, W), 1), 1.0, 0.0).astype(F32)
    first = iota((W, D), 1) < 64
    last_row = iota((W, D), 0) == W - 1
    lam = jnp.zeros((D, D), F32)
    gv = jnp.zeros((8, D), F32)
    gr = jnp.zeros((8, W), F32)
    for i in reversed(range(NB)):
        ce = cum_cols[rows(i), :]
        end = ce[W - 1 : W, :]
        expc, tail, decay = jnp.exp(ce), jnp.exp(end - ce), jnp.exp(end)
        bi, ci, xi = b[rows(i), :], c[rows(i), :], x[rows(i), :]
        ee = dot_tn(err[:, rows(i)], row0, HI)
        gv = gv + jnp.sum((ee * normed[rows(i), :]).reshape(W // 8, 8, D), axis=0)
        dy = ee * unit[rows(i), :]
        lamb = lam.astype(BF16)
        bl = dot_nn(bi, lamb) + dot_nn(bi, parts(lam)[1])
        xt = xi.astype(F32) * tail
        dxi = tail * bl
        dg = None
        dcum = None
        for h in range(2):
            dyh = jnp.where(first == (h == 0), dy, 0.0).astype(BF16)
            gm = gmask[h, rows(i), :]
            dyl = jnp.where(first == (h == 0), dy - dy.astype(BF16).astype(F32), 0.0).astype(BF16)
            dxi = dxi + (dot_tn(gm, dyh) + dot_tn(gm, dyl))
            dgm = dot_nt(dyh, xi) + dot_nt(dyl, xi)
            part = dgm * mask[h, rows(i), :].astype(F32)
            dg = part if dg is None else dg + part
            pair = (dgm * gm.astype(F32)).astype(BF16)
            pick = jnp.where(iota((8, W), 0) == h, 1.0, 0.0).astype(BF16)
            term = dot_nt(pick, pair) - dot_nn(pick, pair)
            dcum = term if dcum is None else dcum + term
        dx[rows(i), :] = dxi
        dgb = dg.astype(BF16)
        dye = (dy * expc).astype(BF16)
        st = state[i]
        dc[rows(i), :] = (dot_nn(dgb, bi) + dot_nt(dye, st.astype(BF16))).astype(dc.dtype)
        db[rows(i), :] = (dot_tn(dgb, ci) + dot_nt(xt.astype(BF16), lamb)).astype(db.dtype)
        through = decay * jnp.sum(st * lam, axis=0, keepdims=True)
        ydy = dy * carried[rows(i), :] + jnp.where(last_row, through, 0.0)
        dcum = dcum + dot_nt(hsel, ydy, HI)
        g = dot_nn(dcum, suffix, HI) + dot_nn(dot_nt(hsel, xt * bl, HI), prefix, HI)
        gstep[:, rows(i)] = -(g * rate[:, 0:1])
        gr = gr - g * step[:, rows(i)]
        lam = decay * lam + (dot_tn(ci, dye) + dot_tn(ci, parts(dy * expc)[1]))
    gvalue[...] = jnp.broadcast_to(jnp.sum(gv, axis=0, keepdims=True), (8, D))
    grate[...] = jnp.broadcast_to(jnp.sum(gr, axis=1, keepdims=True), (8, D))


def attention_backward(q, k, v, p, x, dx, dq_acc, dop, delta, dqkv):
    for i in range(NB):
        do = dx[rows(i), :].astype(BF16)
        dop[rows(i), :] = do
        delta[rows(i), :] = jnp.broadcast_to(
            jnp.sum(do.astype(F32) * x[rows(i), :].astype(F32), axis=1, keepdims=True), (W, D)
        )
    for j in range(NB):
        below = pl.ds(j * W, T - j * W)
        pc = p[below, rows(j)]
        do = dop[below, :]
        de = delta[below, :]
        de = jnp.concatenate([de, de], axis=1)
        ds = (pc.astype(F32) * (dot_nt(do, v[rows(j), :]) - de)).astype(BF16)
        dqkv[2, rows(j), :] = dot_tn(pc, do).astype(BF16)
        dqkv[1, rows(j), :] = (dot_tn(ds, q[below, :]) * SCALE).astype(BF16)
        part = dot_nn(ds, k[rows(j), :])
        if j:
            part = part + dq_acc[below, :]
        dqkv[0, rows(j), :] = (part[:W] * SCALE).astype(BF16)
        if j < NB - 1:
            dq_acc[pl.ds((j + 1) * W, T - (j + 1) * W), :] = part[W:]


def kernel_a(q, k, v, b, c, step, rate, weight,
             p, x, cum_rows, cum_cols, state, mask, gmask, unit, normed, carried, value):
    attention_forward(q, k, v, p, x)
    ssd_forward(x, b, c, step, rate, weight, cum_rows, cum_cols, state, mask, gmask, unit, normed, carried, value)


def kernel_b(err, q, k, v, b, c, step, rate, p, x, cum_rows, cum_cols, state, mask, gmask, unit, normed, carried,
             dqkv, db, dc, gstep, grate, gvalue, dx, dq_acc, dop, delta):
    ssd_backward(err, x, b, c, step, rate, cum_rows, cum_cols, state, mask, gmask, unit, normed, carried,
                 dx, db, dc, gstep, grate, gvalue)
    attention_backward(q, k, v, p, x, dx, dq_acc, dop, delta, dqkv)


def sds(shape, dtype):
    return jax.ShapeDtypeStruct(shape, dtype)


MID = (
    sds((T, T), BF16), sds((T, D), BF16), sds((8, T), F32), sds((T, D), F32),
    sds((NB, D, D), F32), sds((2, T, W), BF16), sds((2, T, W), BF16), sds((T, D), F32), sds((T, D), F32),
    sds((T, D), F32),
)
PARAMS = pltpu.CompilerParams(vmem_limit_bytes=60 * 2**20)
ANYV = pl.BlockSpec(memory_space=pltpu.VMEM)


def run_a(q, k, v, b, c, step, rate, weight):
    return pl.pallas_call(
        kernel_a, out_shape=MID + (sds((8, T), F32),),
        in_specs=[ANYV] * 8, out_specs=[ANYV] * 11, compiler_params=PARAMS, name="forward_heads",
    )(q, k, v, b, c, step, rate, weight)


def run_b(err, q, k, v, b, c, step, rate, mid):
    return pl.pallas_call(
        kernel_b,
        out_shape=(sds((3, T, D), BF16), sds((T, D), BF16), sds((T, D), BF16), sds((8, T), F32), sds((8, D), F32), sds((8, D), F32)),
        in_specs=[ANYV] * 18, out_specs=[ANYV] * 6,
        scratch_shapes=[pltpu.VMEM((T, D), F32), pltpu.VMEM((T, D), F32), pltpu.VMEM((T, D), BF16), pltpu.VMEM((T, D), F32)],
        compiler_params=PARAMS, name="backward_heads",
    )(err, q, k, v, b, c, step, rate, *mid)


def local(qkv, ssd_b, ssd_c, step_size, decay_rate, value_weight, returns, step_labels, lengths):
    me = lax.axis_index("context")
    spread = lax.all_to_all(qkv, "context", split_axis=3, concat_axis=2, tiled=True)
    q, k, v = (spread[i, 0, :, 0, :] for i in range(3))
    both = lax.all_gather(jnp.stack([ssd_b[0], ssd_c[0]]), "context", axis=1, tiled=True)
    b, c = both[0], both[1]
    onehot = (step_labels[0][:, None] == jnp.arange(returns.shape[1], dtype=jnp.int32)[None, :]).astype(F32)
    target_here = jnp.dot(onehot, returns[0], precision=HI)
    steps = lax.all_to_all(step_size[0].T, "context", split_axis=0, concat_axis=1, tiled=True)
    target = lax.all_gather(target_here, "context", axis=0, tiled=True)
    step = jnp.pad(steps, ((0, 6), (0, 0)))
    rate = jnp.pad(jnp.broadcast_to(lax.dynamic_slice(decay_rate, (2 * me,), (2,))[:, None], (2, D)), ((0, 6), (0, 0)))
    weight = jnp.broadcast_to(lax.dynamic_slice(value_weight, (D * me,), (D,)).astype(F32)[None], (8, D))
    *mid, partial = run_a(q, k, v, b, c, step, rate, weight)
    value = lax.psum(partial[0], ("context", "head"))
    my_length = lax.dynamic_index_in_dim(lengths, lax.axis_index("rollout"), 0, keepdims=False)
    valid = (jnp.arange(T, dtype=jnp.int32) < my_length).astype(F32)
    error = (value - target) * valid
    dqkv, db, dc, gstep, grate, gvalue = run_b(jnp.broadcast_to(error[None], (8, T)), q, k, v, b, c, step, rate, mid)
    loss_here = 0.5 * jnp.sum(error * error)
    qkv_grad = lax.all_to_all(dqkv[:, None, :, None, :], "context", split_axis=2, concat_axis=3, tiled=True)
    bc = lax.psum_scatter(jnp.stack([db, dc]), "context", scatter_dimension=1, tiled=True)
    bc = lax.psum(bc, "head").astype(F32)
    small = lax.psum(jnp.concatenate([gvalue[0], grate[:2, 0], loss_here[None]]), "rollout")
    loss = small[130] / jnp.sum(lengths).astype(F32)
    gathered = lax.all_gather(small[:130], "context", axis=0)
    gs = lax.all_to_all(gstep[:2], "context", split_axis=1, concat_axis=0, tiled=True)
    return (
        loss, qkv_grad, bc[0][None], bc[1][None], gs.T[None],
        gathered[:, 128:].reshape(-1), gathered[:, :128].reshape(-1),
    )


def solution(mesh):
    in_specs = (
        P(None, "rollout", "context", "head", None), P("rollout", "context", None), P("rollout", "context", None),
        P("rollout", "context", "head"), P("head"), P("head"), P("rollout", None), P("rollout", "context"), P(),
    )
    out_specs = (
        P(), P(None, "rollout", "context", "head", None), P("rollout", "context", None),
        P("rollout", "context", None), P("rollout", "context", "head"), P("head"), P("head"),
    )
    return jax.shard_map(local, mesh=mesh, in_specs=in_specs, out_specs=out_specs, check_vma=False)
```

```python
import functools
import math

import jax
import jax.numpy as jnp
from jax import lax
from jax.experimental import pallas as pl
from jax.experimental.pallas import tpu as pltpu
from jax.sharding import PartitionSpec as P

NORM_EPS = 1e-05
HI = lax.Precision.HIGHEST
F32 = jnp.float32
BF16 = jnp.bfloat16
T = 2048
W = 256
NB = T // W
D = 128
SCALE = 1.0 / math.sqrt(128.0)
LOG2E = 1.4426950408889634


def dot_nn(a, b, precision=None):
    return lax.dot_general(a, b, (((1,), (0,)), ((), ())), precision=precision, preferred_element_type=F32)


def dot_nt(a, b, precision=None):
    return lax.dot_general(a, b, (((1,), (1,)), ((), ())), precision=precision, preferred_element_type=F32)


def dot_tn(a, b, precision=None):
    return lax.dot_general(a, b, (((0,), (0,)), ((), ())), precision=precision, preferred_element_type=F32)


def parts(a):
    high = a.astype(BF16)
    return high, (a - high.astype(F32)).astype(BF16)


def rows(i):
    return pl.ds(i * W, W)


def iota(shape, dim):
    return lax.broadcasted_iota(jnp.int32, shape, dim)


def head_select():
    return jnp.where(iota((8, D), 1) // 64 == iota((8, D), 0), 1.0, 0.0).astype(F32)


def head_mean():
    return jnp.where(iota((D, D), 0) // 64 == iota((D, D), 1) // 64, 1.0 / 64.0, 0.0).astype(F32)


def attention_forward(q, k, v, p, x, arrive):
    causal = iota((W, W), 0) >= iota((W, W), 1)
    c = SCALE * LOG2E
    for i in range(NB):
        arrive(i)
        qi = q[rows(i), :]
        diag = jnp.where(causal, dot_nt(qi, k[rows(i), :]) * c, -1e30)
        top = jnp.max(diag, axis=1, keepdims=True)
        if i:
            past = dot_nt(qi, k[: i * W, :]) * c
            top = jnp.maximum(top, jnp.max(past, axis=1, keepdims=True))
            past = jnp.exp2(past - top)
        diag = jnp.exp2(diag - top)
        total = jnp.sum(diag, axis=1, keepdims=True)
        if i:
            total = total + jnp.sum(past, axis=1, keepdims=True)
        inverse = 1.0 / total
        pd = (diag * inverse).astype(BF16)
        p[rows(i), rows(i)] = pd
        o = dot_nn(pd, v[rows(i), :])
        if i:
            pp = (past * inverse).astype(BF16)
            p[rows(i), : i * W] = pp
            o = o + dot_nn(pp, v[: i * W, :])
        x[rows(i), :] = o.astype(BF16)


def ssd_forward(x, b, c, step, rate, w1, cum_rows, cum_cols, state, mask, gmask, unit, normed, carried, value):
    hsel = head_select()
    hmean = head_mean()
    upto = jnp.where(iota((W, W), 0) <= iota((W, W), 1), 1.0, 0.0).astype(F32)
    causal = iota((W, W), 0) >= iota((W, W), 1)
    first = iota((W, D), 1) < 64
    w8 = jnp.broadcast_to(w1, (8, D))
    st = jnp.zeros((D, D), F32)
    for i in range(NB):
        la = -(step[:, rows(i)] * rate)
        cr = dot_nn(la, upto, HI)
        ce = dot_tn(cr, hsel, HI)
        cum_rows[:, rows(i)] = cr
        cum_cols[rows(i), :] = ce
        end = ce[W - 1 : W, :]
        bi, ci, xi = b[rows(i), :], c[rows(i), :], x[rows(i), :]
        g = dot_nt(ci, bi)
        y = None
        for h in range(2):
            gap = ce[:, 64 * h : 64 * h + 1] - cr[h : h + 1, :]
            m = jnp.exp(jnp.where(causal, gap, -1e30))
            gm = (g * m).astype(BF16)
            mask[h, rows(i), :] = m.astype(BF16)
            gmask[h, rows(i), :] = gm
            xh = jnp.where(first == (h == 0), xi, jnp.zeros_like(xi))
            gl = (g * m - gm.astype(F32)).astype(BF16)
            part = dot_nn(gm, xh) + dot_nn(gl, xh)
            y = part if y is None else y + part
        state[i] = st
        ca = jnp.exp(ce) * (dot_nn(ci, parts(st)[0]) + dot_nn(ci, parts(st)[1]))
        carried[rows(i), :] = ca
        y = y + ca
        xh, xl = parts(xi.astype(F32) * jnp.exp(end - ce))
        st = jnp.exp(end) * st + (dot_tn(bi, xh) + dot_tn(bi, xl))
        r = lax.rsqrt(dot_nn(y * y, hmean, HI) + NORM_EPS)
        n = y * r
        a = dot_nn(n * w1, hmean, HI)
        unit[rows(i), :] = r * (w1 - n * a)
        normed[rows(i), :] = n
        part = dot_nt(w8, n, HI)
        value[2 * i : 2 * i + 1, :] = part[0:1, :D]
        value[2 * i + 1 : 2 * i + 2, :] = part[0:1, D:]


def ssd_backward(err, x, b, c, step, rate, cum_rows, cum_cols, state, mask, gmask, unit, normed, carried,
                 dx, db, dc, gstep):
    hsel = head_select()
    row0 = jnp.where(iota((8, D), 0) == 0, 1.0, 0.0).astype(F32)
    suffix = jnp.where(iota((W, W), 0) >= iota((W, W), 1), 1.0, 0.0).astype(F32)
    prefix = jnp.where(iota((W, W), 0) < iota((W, W), 1), 1.0, 0.0).astype(F32)
    first = iota((W, D), 1) < 64
    last_row = iota((W, D), 0) == W - 1
    lam = jnp.zeros((D, D), F32)
    gv = jnp.zeros((8, D), F32)
    gr = jnp.zeros((8, W), F32)
    for i in reversed(range(NB)):
        ce = cum_cols[rows(i), :]
        end = ce[W - 1 : W, :]
        expc, tail, decay = jnp.exp(ce), jnp.exp(end - ce), jnp.exp(end)
        bi, ci, xi = b[rows(i), :], c[rows(i), :], x[rows(i), :]
        ee = dot_tn(err[:, rows(i)], row0, HI)
        gv = gv + jnp.sum((ee * normed[rows(i), :]).reshape(W // 8, 8, D), axis=0)
        dy = ee * unit[rows(i), :]
        lamb = lam.astype(BF16)
        bl = dot_nn(bi, lamb) + dot_nn(bi, parts(lam)[1])
        xt = xi.astype(F32) * tail
        dxi = tail * bl
        dg = None
        dcum = None
        for h in range(2):
            dyh = jnp.where(first == (h == 0), dy, 0.0).astype(BF16)
            gm = gmask[h, rows(i), :]
            dyl = jnp.where(first == (h == 0), dy - dy.astype(BF16).astype(F32), 0.0).astype(BF16)
            dxi = dxi + (dot_tn(gm, dyh) + dot_tn(gm, dyl))
            dgm = dot_nt(dyh, xi) + dot_nt(dyl, xi)
            part = dgm * mask[h, rows(i), :].astype(F32)
            dg = part if dg is None else dg + part
            pair = (dgm * gm.astype(F32)).astype(BF16)
            pick = jnp.where(iota((8, W), 0) == h, 1.0, 0.0).astype(BF16)
            term = dot_nt(pick, pair) - dot_nn(pick, pair)
            dcum = term if dcum is None else dcum + term
        dx[rows(i), :] = dxi
        dgb = dg.astype(BF16)
        dye = (dy * expc).astype(BF16)
        st = state[i]
        dc[rows(i), :] = (dot_nn(dgb, bi) + dot_nt(dye, st.astype(BF16))).astype(dc.dtype)
        db[rows(i), :] = (dot_tn(dgb, ci) + dot_nt(xt.astype(BF16), lamb)).astype(db.dtype)
        through = decay * jnp.sum(st * lam, axis=0, keepdims=True)
        ydy = dy * carried[rows(i), :] + jnp.where(last_row, through, 0.0)
        dcum = dcum + dot_nt(hsel, ydy, HI)
        g = dot_nn(dcum, suffix, HI) + dot_nn(dot_nt(hsel, xt * bl, HI), prefix, HI)
        gstep[:, rows(i)] = -(g * rate)
        gr = gr - g * step[:, rows(i)]
        lam = decay * lam + (dot_tn(ci, dye) + dot_tn(ci, parts(dy * expc)[1]))
    return jnp.sum(gv, axis=0, keepdims=True), jnp.sum(gr, axis=1, keepdims=True)


def attention_backward(q, k, v, p, x, dx, dq_acc, dop, delta, dqkv, leave):
    for i in range(NB):
        do = dx[rows(i), :].astype(BF16)
        dop[rows(i), :] = do
        delta[rows(i), :] = jnp.broadcast_to(
            jnp.sum(do.astype(F32) * x[rows(i), :].astype(F32), axis=1, keepdims=True), (W, D)
        )
    for j in range(NB):
        below = pl.ds(j * W, T - j * W)
        pc = p[below, rows(j)]
        do = dop[below, :]
        de = delta[below, :]
        de = jnp.concatenate([de, de], axis=1)
        ds = (pc.astype(F32) * (dot_nt(do, v[rows(j), :]) - de)).astype(BF16)
        dqkv[2, rows(j), :] = dot_tn(pc, do).astype(BF16)
        dqkv[1, rows(j), :] = (dot_tn(ds, q[below, :]) * SCALE).astype(BF16)
        part = dot_nn(ds, k[rows(j), :])
        if j:
            part = part + dq_acc[below, :]
        dqkv[0, rows(j), :] = (part[:W] * SCALE).astype(BF16)
        if j < NB - 1:
            dq_acc[pl.ds((j + 1) * W, T - (j + 1) * W), :] = part[W:]
        leave(j)


MESH = pl.DeviceIdType.MESH
CTX = 16
TOK = 128


def put(src, dst, sems, slot_out, slot_in, **where):
    return pltpu.make_async_remote_copy(
        src_ref=src, dst_ref=dst, send_sem=sems.at[0, slot_out], recv_sem=sems.at[1, slot_in],
        device_id=where, device_id_type=MESH,
    )


def block(i):
    return pl.ds(pl.multiple_of(i * TOK, TOK), TOK)


def others(me, act):
    def body(o, carry):
        act(lax.rem(me + o, CTX))
        return carry

    lax.fori_loop(1, CTX, body, 0)


def heads_kernel(qkv_in, b_in, c_in, step_in, labels, table, rate_in, weight_in, lengths,
                 dqkv_out, gb_out, gc_out, gstep_out, small_out,
                 stage, qkv, bc, aux_out, aux, p, x, cum_rows, cum_cols, state, mask, gmask, unit, normed, carried,
                 vpart, vpair, vchip, vall, err, dx, dq_acc, dop, delta, dqkv, dbc, dpair, dsum, dall, gres, gother,
                 gstep, gs_in, small, small_x, small_sum, small_all, land,
                 s_qkv, s_bc, s_aux, s_vp, s_v, s_dp, s_d, s_g, s_gs, s_x, s_sm, s_out):
    me = lax.axis_index("context")
    core = lax.axis_index("head")
    rollout = lax.axis_index("rollout")
    twin = 1 - core
    barrier = pltpu.get_barrier_semaphore()
    others(me, lambda d: pl.semaphore_signal(barrier, inc=1, device_id={"context": d}, device_id_type=MESH))
    pl.semaphore_signal(barrier, inc=1, device_id={"head": twin}, device_id_type=MESH)
    for o in range(1, 4):
        pl.semaphore_signal(barrier, inc=1, device_id={"rollout": lax.rem(rollout + o, 4)}, device_id_type=MESH)

    for i in range(3):
        stage[:, i] = jnp.swapaxes(qkv_in[i], 0, 1)
    onehot = jnp.where(iota((64, TOK), 0) == labels[...], 1.0, 0.0).astype(F32)
    target = dot_nn(jnp.broadcast_to(table[...], (8, 64)), onehot, HI)[0:1]
    steps = jnp.concatenate([step_in[...], jnp.zeros((TOK, 96), F32)], axis=1).T
    for d in range(CTX):
        aux_out[d] = jnp.concatenate([steps[2 * d : 2 * d + 2], target, jnp.zeros((5, TOK), F32)], axis=0)
    pl.semaphore_wait(barrier, CTX + 3)

    def send_qkv(d):
        return put(stage.at[d], qkv.at[:, block(me)], s_qkv, d, me, context=d)

    def send_b(d):
        return put(b_in, bc.at[0, block(me)], s_bc, d, me, context=d)

    def send_c(d):
        return put(c_in, bc.at[1, block(me)], s_bc, CTX + d, CTX + me, context=d)

    def send_aux(d):
        return put(aux_out.at[d], aux.at[:, block(me)], s_aux, d, me, context=d)

    others(me, lambda d: send_qkv(d).start())

    def send_rest(d):
        send_aux(d).start()
        send_b(d).start()
        send_c(d).start()

    others(me, send_rest)
    qkv[:, block(me)] = stage[me]
    bc[0, block(me)] = b_in[...]
    bc[1, block(me)] = c_in[...]
    aux[:, block(me)] = aux_out[me]

    def arrive(i):
        for s in (2 * i, 2 * i + 1):
            @pl.when(me != s)
            def _():
                put(stage.at[s], qkv.at[:, block(s)], s_qkv, s, s, context=s).wait_recv()

    attention_forward(qkv.at[0], qkv.at[1], qkv.at[2], p, x, arrive)

    def got_rest(s):
        put(aux_out.at[s], aux.at[:, block(s)], s_aux, s, s, context=s).wait_recv()
        put(b_in, bc.at[0, block(s)], s_bc, s, s, context=s).wait_recv()
        put(c_in, bc.at[1, block(s)], s_bc, CTX + s, CTX + s, context=s).wait_recv()

    others(me, got_rest)
    rate = jnp.sum(
        jnp.where((iota((8, 32), 1) == 2 * me + iota((8, 32), 0)) & (iota((8, 32), 0) < 2), rate_in[...], 0.0),
        axis=1, keepdims=True,
    )
    w1 = jnp.sum(jnp.where(iota((CTX, D), 0) == me, weight_in[...].astype(F32), 0.0), axis=0, keepdims=True)
    b, c = bc.at[0], bc.at[1]
    ssd_forward(x, b, c, aux, rate, w1, cum_rows, cum_cols, state, mask, gmask, unit, normed, carried, vpart)

    pair = put(vpart, vpair, s_vp, 0, 0, head=twin)
    pair.start()
    pair.wait_recv()
    vchip[...] = vpart[...] + vpair[...]
    vall[me] = vchip[...]
    others(me, lambda d: put(vchip, vall.at[me], s_v, d, me, context=d).start())
    others(me, lambda s: put(vchip, vall.at[s], s_v, s, s, context=s).wait_recv())
    value = vall[0]
    for s in range(1, CTX):
        value = value + vall[s]
    limit = lengths[rollout]
    loss = jnp.zeros((1, TOK), F32)
    for s in range(CTX):
        valid = jnp.where(iota((1, TOK), 1) + s * TOK < limit, 1.0, 0.0).astype(F32)
        e = (value[s : s + 1] - aux[2:3, s * TOK : (s + 1) * TOK]) * valid
        loss = loss + e * e
        err[:, s * TOK : (s + 1) * TOK] = jnp.broadcast_to(e, (8, TOK))

    gv, gr = ssd_backward(err, x, b, c, aux, rate, cum_rows, cum_cols, state, mask, gmask, unit, normed, carried,
                          dx, dbc.at[0], dbc.at[1], gstep)
    pair_d = put(dbc.at[twin], dpair, s_dp, 0, 0, head=twin)
    pair_d.start()
    small[...] = jnp.concatenate(
        [gv, jnp.broadcast_to(gr[0:1], (1, D)), jnp.broadcast_to(gr[1:2], (1, D)),
         jnp.broadcast_to(0.5 * jnp.sum(loss, axis=1, keepdims=True), (1, D)), jnp.zeros((4, D), F32)], axis=0)
    small_x[rollout] = small[...]

    def send_x(o):
        d = lax.rem(rollout + o, 4)
        return put(small, small_x.at[rollout], s_x, d, rollout, rollout=d)

    for o in range(1, 4):
        send_x(o).start()

    def send_gs(d):
        return put(gstep.at[:, block(d)], gs_in.at[me], s_gs, d, me, context=d)

    others(me, lambda d: send_gs(d).start())
    gs_in[me] = gstep[:, block(me)]

    def send_out(d):
        return put(dqkv.at[:, block(d)], land.at[me], s_out, d, me, context=d)

    def send_d(d):
        return put(dsum.at[block(d)], dall.at[me], s_d, d, me, context=d)

    def send_small(d):
        return put(small_sum, small_all.at[me], s_sm, d, me, context=d)

    def leave(j):
        for d in (2 * j, 2 * j + 1):
            @pl.when(me != d)
            def _():
                send_out(d).start()
        if j == 0:
            pair_d.wait_recv()
            dsum[...] = (dbc[core].astype(F32) + dpair[...].astype(F32)).astype(BF16)
            others(me, lambda d: send_d(d).start())
            dall[me] = dsum[block(me)]
            for o in range(1, 4):
                d = lax.rem(rollout + o, 4)
                put(small, small_x.at[d], s_x, d, d, rollout=d).wait_recv()
            small_sum[...] = (small_x[0] + small_x[1]) + (small_x[2] + small_x[3])
            others(me, lambda d: send_small(d).start())
            small_all[me] = small_sum[...]

    attention_backward(qkv.at[0], qkv.at[1], qkv.at[2], p, x, dx, dq_acc, dop, delta, dqkv, leave)
    land[me] = dqkv[:, block(me)]

    others(me, lambda s: put(dsum.at[block(s)], dall.at[s], s_d, s, s, context=s).wait_recv())
    total = dall[0].astype(F32)
    for s in range(1, CTX):
        total = total + dall[s].astype(F32)
    gres[...] = total
    swap = put(gres, gother, s_g, 0, 0, head=twin)
    swap.start()
    others(me, lambda s: put(gstep.at[:, block(s)], gs_in.at[s], s_gs, s, s, context=s).wait_recv())
    gs = jnp.concatenate([gs_in[s, 0:2] for s in range(CTX)] + [jnp.zeros((96, TOK), F32)], axis=0).T
    gstep_out[...] = gs[:, :32]
    others(me, lambda s: put(small_sum, small_all.at[s], s_sm, s, s, context=s).wait_recv())
    small_out[...] = small_all[...]
    swap.wait_recv()
    mine, other = gres[...], gother[...]
    gb_out[...] = jnp.where(core == 0, mine, other)
    gc_out[...] = jnp.where(core == 0, other, mine)
    others(me, lambda s: put(dqkv.at[:, block(s)], land.at[s], s_out, s, s, context=s).wait_recv())
    for i in range(3):
        dqkv_out[i] = jnp.swapaxes(land[:, i], 0, 1)

    def sent(d):
        send_qkv(d).wait_send()
        send_aux(d).wait_send()
        send_b(d).wait_send()
        send_c(d).wait_send()
        put(vchip, vall.at[me], s_v, d, me, context=d).wait_send()
        send_gs(d).wait_send()
        send_d(d).wait_send()
        send_small(d).wait_send()
        send_out(d).wait_send()

    others(me, sent)
    for o in range(1, 4):
        send_x(o).wait_send()
    pair.wait_send()
    pair_d.wait_send()
    swap.wait_send()


def sds(shape, dtype):
    return jax.ShapeDtypeStruct(shape, dtype)


def vmem(*shape, dtype=F32):
    return pltpu.VMEM(shape, dtype)


def dma(n):
    return pltpu.SemaphoreType.DMA((2, n))


def run_heads(*args):
    whole = pl.BlockSpec(memory_space=pltpu.VMEM)
    return pl.pallas_call(
        heads_kernel,
        out_shape=(sds((3, TOK, CTX, D), BF16), sds((TOK, D), F32), sds((TOK, D), F32), sds((TOK, 32), F32),
                   sds((CTX, 8, D), F32)),
        in_specs=[whole] * 8 + [pl.BlockSpec(memory_space=pltpu.SMEM)],
        out_specs=[whole] * 5,
        scratch_shapes=[
            vmem(CTX, 3, TOK, D, dtype=BF16), vmem(3, T, D, dtype=BF16), vmem(2, T, D, dtype=BF16),
            vmem(CTX, 8, TOK), vmem(8, T), vmem(T, T, dtype=BF16), vmem(T, D, dtype=BF16), vmem(8, T), vmem(T, D),
            vmem(NB, D, D), vmem(2, T, W, dtype=BF16), vmem(2, T, W, dtype=BF16), vmem(T, D), vmem(T, D), vmem(T, D),
            vmem(CTX, TOK), vmem(CTX, TOK), vmem(CTX, TOK), vmem(CTX, CTX, TOK), vmem(8, T),
            vmem(T, D), vmem(T, D), vmem(T, D, dtype=BF16), vmem(T, D), vmem(3, T, D, dtype=BF16),
            vmem(2, T, D, dtype=BF16), vmem(T, D, dtype=BF16), vmem(T, D, dtype=BF16), vmem(CTX, TOK, D, dtype=BF16),
            vmem(TOK, D), vmem(TOK, D), vmem(8, T), vmem(CTX, 8, TOK), vmem(8, D), vmem(4, 8, D), vmem(8, D),
            vmem(CTX, 8, D), vmem(CTX, 3, TOK, D, dtype=BF16),
            dma(CTX), dma(2 * CTX), dma(CTX), dma(1), dma(CTX), dma(1), dma(CTX), dma(1), dma(CTX), dma(4), dma(CTX),
            dma(CTX),
        ],
        compiler_params=pltpu.CompilerParams(vmem_limit_bytes=60 * 2**20, collective_id=0, has_side_effects=True),
        name="heads",
    )(*args)


def local(qkv, ssd_b, ssd_c, step_size, decay_rate, value_weight, returns, step_labels, lengths):
    dqkv, gb, gc, gstep, small = run_heads(
        qkv[:, 0], ssd_b[0], ssd_c[0], step_size[0], step_labels, returns, decay_rate[None],
        value_weight.reshape(CTX, D), lengths)
    loss = small[0, 3, 0] / jnp.sum(lengths).astype(F32)
    return (loss, dqkv[:, None], gb[None], gc[None], gstep[None], small[:, 1:3, 0].reshape(-1), small[:, 0].reshape(-1))


def solution(mesh):
    in_specs = (
        P(None, "rollout", "context", "head", None), P("rollout", "context", None), P("rollout", "context", None),
        P("rollout", "context", "head"), P("head"), P("head"), P("rollout", None), P("rollout", "context"), P(),
    )
    out_specs = (
        P(), P(None, "rollout", "context", "head", None), P("rollout", "context", None),
        P("rollout", "context", None), P("rollout", "context", "head"), P("head"), P("head"),
    )
    return jax.shard_map(local, mesh=mesh, in_specs=in_specs, out_specs=out_specs, check_vma=False)
```

```python
import functools
import math

import jax
import jax.numpy as jnp
from jax import lax
from jax.experimental import pallas as pl
from jax.experimental.pallas import tpu as pltpu
from jax.sharding import PartitionSpec as P

NORM_EPS = 1e-05
HI = lax.Precision.HIGHEST
F32 = jnp.float32
BF16 = jnp.bfloat16
T = 2048
W = 256
NB = T // W
D = 128
SCALE = 1.0 / math.sqrt(128.0)
LOG2E = 1.4426950408889634


def dot_nn(a, b, precision=None):
    return lax.dot_general(a, b, (((1,), (0,)), ((), ())), precision=precision, preferred_element_type=F32)


def dot_nt(a, b, precision=None):
    return lax.dot_general(a, b, (((1,), (1,)), ((), ())), precision=precision, preferred_element_type=F32)


def dot_tn(a, b, precision=None):
    return lax.dot_general(a, b, (((0,), (0,)), ((), ())), precision=precision, preferred_element_type=F32)


def parts3(a):
    high = a.astype(BF16).astype(F32)
    mid = (a - high).astype(BF16).astype(F32)
    low = a - high - mid
    return jnp.concatenate([high, mid, low, jnp.zeros_like(a)], axis=0).astype(BF16)


def wide(a):
    high, low = parts(a)
    return jnp.concatenate([high, low], axis=1)


def fold(a):
    return a[:, :D] + a[:, D:]


def parts(a):
    high = a.astype(BF16)
    return high, (a - high.astype(F32)).astype(BF16)


def rows(i):
    return pl.ds(i * W, W)


def iota(shape, dim):
    return lax.broadcasted_iota(jnp.int32, shape, dim)


def head_select():
    return jnp.where(iota((8, D), 1) // 64 == iota((8, D), 0), 1.0, 0.0).astype(F32)


def head_mean():
    return jnp.where(iota((D, D), 0) // 64 == iota((D, D), 1) // 64, 1.0 / 64.0, 0.0).astype(F32)


def attention_forward(q, k, v, p, x, arrive):
    causal = iota((W, W), 0) >= iota((W, W), 1)
    c = SCALE * LOG2E
    for i in range(NB):
        arrive(i)
        qi = q[rows(i), :]
        diag = jnp.where(causal, dot_nt(qi, k[rows(i), :]) * c, -1e30)
        top = jnp.max(diag, axis=1, keepdims=True)
        if i:
            past = dot_nt(qi, k[: i * W, :]) * c
            top = jnp.maximum(top, jnp.max(past, axis=1, keepdims=True))
            past = jnp.exp2(past - top)
        diag = jnp.exp2(diag - top)
        total = jnp.sum(diag, axis=1, keepdims=True)
        if i:
            total = total + jnp.sum(past, axis=1, keepdims=True)
        inverse = 1.0 / total
        pd = (diag * inverse).astype(BF16)
        p[rows(i), rows(i)] = pd
        o = dot_nn(pd, v[rows(i), :])
        if i:
            pp = (past * inverse).astype(BF16)
            p[rows(i), : i * W] = pp
            o = o + dot_nn(pp, v[: i * W, :])
        x[rows(i), :] = o.astype(BF16)


def ssd_prepare(b, c, step, rate, cum_rows, cum_cols, mask, gmask, glow):
    upto = jnp.where(iota((W, W), 0) <= iota((W, W), 1), 1.0, 0.0).astype(BF16)
    causal = iota((W, W), 0) >= iota((W, W), 1)
    hsel = head_select()
    hsel4 = jnp.concatenate([hsel] * 4, axis=0).astype(BF16)
    la = jnp.concatenate([-(step[:, rows(i)] * rate) for i in range(NB)], axis=0)
    sums = dot_nn(parts3(la), upto)
    sums = sums[: 8 * NB] + sums[8 * NB : 16 * NB] + sums[16 * NB : 24 * NB]
    for i in range(NB):
        cr = sums[8 * i : 8 * i + 8]
        ce = dot_tn(parts3(cr), hsel4)
        cum_rows[:, rows(i)] = cr
        cum_cols[rows(i), :] = ce
        g = dot_nt(c[rows(i), :], b[rows(i), :])
        for h in range(2):
            gap = ce[:, 64 * h : 64 * h + 1] - cr[h : h + 1, :]
            m = jnp.exp(jnp.where(causal, gap, -1e30))
            high, low = parts(g * m)
            mask[h, rows(i), :] = m.astype(BF16)
            gmask[h, rows(i), :] = high
            glow[h, rows(i), :] = low


def ssd_forward(x, b, c, w1, cum_cols, state, gmask, glow, unit, normed, carried, value):
    hmean = head_mean().astype(BF16)
    first = iota((W, D), 1) < 64
    w8 = jnp.broadcast_to(w1, (8, D)).astype(BF16)
    st = jnp.zeros((D, D), F32)

    def mean(a):
        high, low = parts(a)
        return dot_nn(high, hmean) + dot_nn(low, hmean)

    for i in range(NB):
        ce = cum_cols[rows(i), :]
        end = ce[W - 1 : W, :]
        bi, ci, xi = b[rows(i), :], c[rows(i), :], x[rows(i), :]
        state[i] = st
        ca = jnp.exp(ce) * fold(dot_nn(ci, wide(st)))
        carried[rows(i), :] = ca
        y = ca
        for h in range(2):
            xh = jnp.where(first == (h == 0), xi, jnp.zeros_like(xi))
            y = y + dot_nn(gmask[h, rows(i), :], xh) + dot_nn(glow[h, rows(i), :], xh)
        st = jnp.exp(end) * st + fold(dot_tn(bi, wide(xi.astype(F32) * jnp.exp(end - ce))))
        r = lax.rsqrt(mean(y * y) + NORM_EPS)
        n = y * r
        unit[rows(i), :] = r * (w1 - n * mean(n * w1))
        normed[rows(i), :] = n
        high, low = parts(n)
        part = dot_nt(w8, high) + dot_nt(w8, low)
        value[2 * i : 2 * i + 1, :] = part[0:1, :D]
        value[2 * i + 1 : 2 * i + 2, :] = part[0:1, D:]


def ssd_pairs(x, b, cum_cols, state, mask, gmask, unit, carried, pairs, gate, across, dcp):
    hselb = head_select().astype(BF16)
    first = iota((W, D), 1) < 64
    for i in range(NB):
        xi, u = x[rows(i), :], unit[rows(i), :]
        dg, row = None, None
        for h in range(2):
            high, low = parts(jnp.where(first == (h == 0), u, 0.0))
            ux = dot_nt(high, xi) + dot_nt(low, xi)
            part = ux * mask[h, rows(i), :].astype(F32)
            dg = part if dg is None else dg + part
            pair = (ux * gmask[h, rows(i), :].astype(F32)).astype(BF16)
            pairs[h, rows(i), :] = pair
            pick = jnp.where(iota((8, W), 0) == h, 1.0, 0.0).astype(BF16)
            term = dot_nt(pick, pair)
            row = term if row is None else row + term
        dgb = dg.astype(BF16)
        gate[rows(i), :] = dgb
        high, low = parts(u * carried[rows(i), :])
        across[:, rows(i)] = row + dot_nt(hselb, high) + dot_nt(hselb, low)
        ue = (u * jnp.exp(cum_cols[rows(i), :])).astype(BF16)
        dcp[rows(i), :] = dot_nn(dgb, b[rows(i), :]) + dot_nt(ue, state[i].astype(BF16))


def ssd_back_step(i, lam, gv, err, ecol, x, b, c, cum_cols, state, gmask, unit, normed, pairs, gate, across, dcp,
                  dx, db, dc, sums, cross):
    hsel = head_select()
    first = iota((W, D), 1) < 64
    ce = cum_cols[rows(i), :]
    end = ce[W - 1 : W, :]
    expc, tail, decay = jnp.exp(ce), jnp.exp(end - ce), jnp.exp(end)
    bi, ci, xi = b[rows(i), :], c[rows(i), :], x[rows(i), :]
    ee, er = ecol[rows(i), :], err[:, rows(i)]
    dy = ee * unit[rows(i), :]
    bl = fold(dot_nn(bi, wide(lam)))
    xt = xi.astype(F32) * tail
    dxi = tail * bl
    col = None
    for h in range(2):
        gm = gmask[h, rows(i), :]
        dxi = dxi + fold(dot_tn(gm, wide(jnp.where(first == (h == 0), dy, 0.0))))
        eh = jnp.where(iota((8, W), 0) == h, er, 0.0)
        high = eh.astype(BF16).astype(F32)
        two = dot_nn(jnp.concatenate([high, eh - high], axis=0).astype(BF16), pairs[h, rows(i), :])
        two = two[:8] + two[8:]
        col = two if col is None else col + two
    dx[rows(i), :] = dxi
    st = state[i]
    dc[rows(i), :] = (ee * dcp[rows(i), :]).astype(BF16)
    db[rows(i), :] = (
        dot_tn(gate[rows(i), :], (ee * ci.astype(F32)).astype(BF16)) + dot_nt(xt.astype(BF16), lam.astype(BF16))
    ).astype(BF16)
    through = jnp.sum(hsel * (decay * jnp.sum(st * lam, axis=0, keepdims=True)), axis=1, keepdims=True)
    sums[8 * i : 8 * i + 8, :] = er * across[:, rows(i)] - col + jnp.where(iota((8, W), 1) == W - 1, through, 0.0)
    high, low = parts(xt * bl)
    hselb = hsel.astype(BF16)
    cross[8 * i : 8 * i + 8, :] = dot_nt(hselb, high) + dot_nt(hselb, low)
    gv = gv + jnp.sum((ee * normed[rows(i), :]).reshape(W // 8, 8, D), axis=0)
    lam = decay * lam + fold(dot_tn(ci, wide(dy * expc)))
    return lam, gv


def ssd_finish(step, rate, sums, cross, gstep):
    suffix = jnp.where(iota((W, W), 0) >= iota((W, W), 1), 1.0, 0.0).astype(BF16)
    prefix = jnp.where(iota((W, W), 0) < iota((W, W), 1), 1.0, 0.0).astype(BF16)
    g = dot_nn(parts3(sums[...]), suffix) + dot_nn(parts3(cross[...]), prefix)
    g = g[: 8 * NB] + g[8 * NB : 16 * NB] + g[16 * NB : 24 * NB]
    gr = jnp.zeros((8, W), F32)
    for i in range(NB):
        gi = g[8 * i : 8 * i + 8]
        gstep[:, rows(i)] = -(gi * rate)
        gr = gr - gi * step[:, rows(i)]
    return jnp.sum(gr, axis=1, keepdims=True)


def attention_back_step(i, q, k, v, p, x, dx, dk_acc, dv_acc, dqkv):
    n = (i + 1) * W
    do = dx[rows(i), :].astype(BF16)
    delta = jnp.sum(do.astype(F32) * x[rows(i), :].astype(F32), axis=1, keepdims=True)
    pi = p[rows(i), :n]
    qi = q[rows(i), :]
    ds = (pi.astype(F32) * (dot_nt(do, v[:n, :]) - delta)).astype(BF16)
    dqkv[0, rows(i), :] = (dot_nn(ds, k[:n, :]) * SCALE).astype(BF16)
    dk = dot_tn(ds, qi)
    dv = dot_tn(pi, do)
    if i < NB - 1:
        dk = dk + dk_acc[:n, :]
        dv = dv + dv_acc[:n, :]
    if i:
        dk_acc[: n - W, :] = dk[: n - W]
        dv_acc[: n - W, :] = dv[: n - W]
    dqkv[1, rows(i), :] = (dk[n - W :] * SCALE).astype(BF16)
    dqkv[2, rows(i), :] = dv[n - W :].astype(BF16)


MESH = pl.DeviceIdType.MESH
CTX = 16
TOK = 128


def put(src, dst, sems, slot_out, slot_in, **where):
    return pltpu.make_async_remote_copy(
        src_ref=src, dst_ref=dst, send_sem=sems.at[0, slot_out], recv_sem=sems.at[1, slot_in],
        device_id=where, device_id_type=MESH,
    )


def block(i):
    return pl.ds(pl.multiple_of(i * TOK, TOK), TOK)


def others(me, act):
    def body(o, carry):
        act(lax.rem(me + o, CTX))
        return carry

    lax.fori_loop(1, CTX, body, 0)


def heads_kernel(qkv_in, b_in, c_in, step_in, labels, table, rate_in, weight_in, lengths,
                 land_out, gb_out, gc_out, gs_out, small_out,
                 stage, qkv, bc, aux_out, aux, p, x, cum_rows, cum_cols, state, mask, gmask, glow, unit, normed, carried,
                 pairs, gate, across, dcp, vpart, vpair, vchip, vall, err, ecol, dx, dk_acc, dv_acc, dqkv,
                 dbc, dpair, dsum, dall, gres, gother, sums, cross, gstep, gs_in, small, small_x, small_sum, small_all,
                 land, s_qkv, s_bc, s_twin, s_aux, s_vp, s_v, s_dp, s_d, s_g, s_gs, s_x, s_sm, s_out):
    me = lax.axis_index("context")
    core = lax.axis_index("head")
    rollout = lax.axis_index("rollout")
    twin = 1 - core
    barrier = pltpu.get_barrier_semaphore()
    others(me, lambda d: pl.semaphore_signal(barrier, inc=1, device_id={"context": d}, device_id_type=MESH))
    pl.semaphore_signal(barrier, inc=1, device_id={"head": twin}, device_id_type=MESH)
    for o in range(1, 4):
        pl.semaphore_signal(barrier, inc=1, device_id={"rollout": lax.rem(rollout + o, 4)}, device_id_type=MESH)

    onehot = jnp.where(iota((64, TOK), 0) == labels[...], 1.0, 0.0).astype(F32)
    target = dot_nn(jnp.broadcast_to(table[...], (8, 64)), onehot, HI)[0:1]
    for d in range(CTX):
        aux_out[d] = jnp.concatenate([step_in[2 * d : 2 * d + 2, :], target, jnp.zeros((5, TOK), F32)], axis=0)
    bc[0, block(me)] = b_in[...]
    bc[1, block(me)] = c_in[...]
    pl.semaphore_wait(barrier, CTX + 3)

    def send_aux(d):
        return put(aux_out.at[d], aux.at[:, block(me)], s_aux, d, me, context=d)

    def send_bc(d):
        return put(bc.at[core, block(me)], bc.at[core, block(me)], s_bc, d, me, context=d)

    def send_qkv(d):
        return put(stage.at[d], qkv.at[:, block(me)], s_qkv, d, me, context=d)

    def send_early(d):
        send_bc(d).start()
        send_aux(d).start()

    others(me, send_early)
    for i in range(3):
        stage[:, i] = jnp.swapaxes(qkv_in[i], 0, 1)
    others(me, lambda d: send_qkv(d).start())
    qkv[:, block(me)] = stage[me]
    aux[:, block(me)] = aux_out[me]
    rate = jnp.sum(
        jnp.where((iota((8, 32), 1) == 2 * me + iota((8, 32), 0)) & (iota((8, 32), 0) < 2), rate_in[...], 0.0),
        axis=1, keepdims=True,
    )
    w1 = jnp.sum(jnp.where(iota((CTX, D), 0) == me, weight_in[...].astype(F32), 0.0), axis=0, keepdims=True)

    def got_bc(s):
        put(bc.at[core, block(s)], bc.at[core, block(s)], s_bc, s, s, context=s).wait_recv()

    others(me, got_bc)

    def send_twin(s):
        return put(bc.at[core, block(s)], bc.at[core, block(s)], s_twin, s, s, head=twin)

    others(me, lambda s: send_twin(s).start())
    others(me, lambda s: put(aux_out.at[s], aux.at[:, block(s)], s_aux, s, s, context=s).wait_recv())
    others(me, lambda s: put(bc.at[twin, block(s)], bc.at[twin, block(s)], s_twin, s, s, head=twin).wait_recv())
    b, c = bc.at[0], bc.at[1]
    ssd_prepare(b, c, aux, rate, cum_rows, cum_cols, mask, gmask, glow)

    def arrive(i):
        for s in (2 * i, 2 * i + 1):
            @pl.when(me != s)
            def _():
                put(stage.at[s], qkv.at[:, block(s)], s_qkv, s, s, context=s).wait_recv()

    attention_forward(qkv.at[0], qkv.at[1], qkv.at[2], p, x, arrive)
    ssd_forward(x, b, c, w1, cum_cols, state, gmask, glow, unit, normed, carried, vpart)

    pair = put(vpart, vpair, s_vp, 0, 0, head=twin)
    pair.start()
    pair.wait_recv()
    vchip[...] = vpart[...] + vpair[...]
    vall[me] = vchip[...]
    others(me, lambda d: put(vchip, vall.at[me], s_v, d, me, context=d).start())
    ssd_pairs(x, b, cum_cols, state, mask, gmask, unit, carried, pairs, gate, across, dcp)
    others(me, lambda s: put(vchip, vall.at[s], s_v, s, s, context=s).wait_recv())
    value = vall[0]
    for s in range(1, CTX):
        value = value + vall[s]
    limit = lengths[rollout]
    loss = jnp.zeros((1, TOK), F32)
    for s in range(CTX):
        valid = jnp.where(iota((1, TOK), 1) + s * TOK < limit, 1.0, 0.0).astype(F32)
        e = (value[s : s + 1] - aux[2:3, s * TOK : (s + 1) * TOK]) * valid
        loss = loss + e * e
        err[:, s * TOK : (s + 1) * TOK] = jnp.broadcast_to(e, (8, TOK))
    row0 = jnp.where(iota((8, D), 0) == 0, 1.0, 0.0).astype(F32)
    ecol[...] = dot_tn(parts3(err[...]), jnp.concatenate([row0] * 4, axis=0).astype(BF16))

    def send_pair(i):
        return put(dbc.at[twin, rows(i)], dpair.at[rows(i)], s_dp, i, i, head=twin)

    def send_d(d):
        return put(dsum.at[block(d)], dall.at[me], s_d, d, me, context=d)

    def send_out(d):
        return put(dqkv.at[:, block(d)], land.at[me], s_out, d, me, context=d)

    q, k, v = qkv.at[0], qkv.at[1], qkv.at[2]
    lam = jnp.zeros((D, D), F32)
    gv = jnp.zeros((8, D), F32)
    for i in reversed(range(NB)):
        lam, gv = ssd_back_step(i, lam, gv, err, ecol, x, b, c, cum_cols, state, gmask, unit, normed, pairs, gate,
                                across, dcp, dx, dbc.at[0], dbc.at[1], sums, cross)
        send_pair(i).start()
        attention_back_step(i, q, k, v, p, x, dx, dk_acc, dv_acc, dqkv)
        for d in (2 * i, 2 * i + 1):
            @pl.when(me != d)
            def _():
                send_out(d).start()
        send_pair(i).wait_recv()
        dsum[rows(i), :] = (dbc[core, rows(i), :].astype(F32) + dpair[rows(i), :].astype(F32)).astype(BF16)
        for d in (2 * i, 2 * i + 1):
            @pl.when(me != d)
            def _():
                send_d(d).start()

    gr = ssd_finish(aux, rate, sums, cross, gstep)
    small[...] = jnp.concatenate(
        [jnp.sum(gv, axis=0, keepdims=True), jnp.broadcast_to(gr[0:1], (1, D)), jnp.broadcast_to(gr[1:2], (1, D)),
         jnp.broadcast_to(0.5 * jnp.sum(loss, axis=1, keepdims=True), (1, D)), jnp.zeros((4, D), F32)], axis=0)
    small_x[rollout] = small[...]

    def send_x(o):
        d = lax.rem(rollout + o, 4)
        return put(small, small_x.at[rollout], s_x, d, rollout, rollout=d)

    for o in range(1, 4):
        send_x(o).start()

    def send_gs(d):
        return put(gstep.at[:, block(d)], gs_in.at[me], s_gs, d, me, context=d)

    def send_small(d):
        return put(small_sum, small_all.at[me], s_sm, d, me, context=d)

    others(me, lambda d: send_gs(d).start())
    gs_in[me] = gstep[:, block(me)]
    dall[me] = dsum[block(me)]
    land[me] = dqkv[:, block(me)]
    for o in range(1, 4):
        d = lax.rem(rollout + o, 4)
        put(small, small_x.at[d], s_x, d, d, rollout=d).wait_recv()
    small_sum[...] = (small_x[0] + small_x[1]) + (small_x[2] + small_x[3])
    others(me, lambda d: send_small(d).start())
    small_all[me] = small_sum[...]

    others(me, lambda s: put(dsum.at[block(s)], dall.at[s], s_d, s, s, context=s).wait_recv())
    total = dall[0].astype(F32)
    for s in range(1, CTX):
        total = total + dall[s].astype(F32)
    gres[...] = total
    swap = put(gres, gother, s_g, 0, 0, head=twin)
    swap.start()
    others(me, lambda s: put(gstep.at[:, block(s)], gs_in.at[s], s_gs, s, s, context=s).wait_recv())
    gs_out[...] = jnp.concatenate([gs_in[s, 0:2] for s in range(CTX)], axis=0)
    others(me, lambda s: put(small_sum, small_all.at[s], s_sm, s, s, context=s).wait_recv())
    small_out[...] = small_all[...]
    swap.wait_recv()
    mine, other = gres[...], gother[...]
    gb_out[...] = jnp.where(core == 0, mine, other)
    gc_out[...] = jnp.where(core == 0, other, mine)
    others(me, lambda s: put(dqkv.at[:, block(s)], land.at[s], s_out, s, s, context=s).wait_recv())
    land_out[...] = land[...]

    def sent(d):
        send_qkv(d).wait_send()
        send_aux(d).wait_send()
        send_bc(d).wait_send()
        send_twin(d).wait_send()
        put(vchip, vall.at[me], s_v, d, me, context=d).wait_send()
        send_gs(d).wait_send()
        send_d(d).wait_send()
        send_small(d).wait_send()
        send_out(d).wait_send()

    others(me, sent)
    for o in range(1, 4):
        send_x(o).wait_send()
    for i in range(NB):
        send_pair(i).wait_send()
    pair.wait_send()
    swap.wait_send()


def place_kernel(land, gb, gc, gs, small, lengths, dqkv_out, gb_out, gc_out, gs_out, gvalue_out, grate_out, loss_out):
    for i in range(3):
        dqkv_out[i] = jnp.swapaxes(land[:, i], 0, 1)
    gb_out[...] = gb[...]
    gc_out[...] = gc[...]
    gs_out[...] = gs[...]
    gvalue_out[...] = jnp.concatenate([small[s, 0:1] for s in range(CTX)], axis=0)
    lane = iota((1, 32), 1)
    grate = jnp.zeros((1, 32), F32)
    for s in range(CTX):
        for h in range(2):
            grate = jnp.where(lane == 2 * s + h, small[s, 1 + h : 2 + h, 0:32], grate)
    grate_out[...] = grate
    count = lengths[0] + lengths[1] + lengths[2] + lengths[3]
    loss_out[...] = small[0, 3:4, 0:1] / jnp.full((1, 1), count, jnp.int32).astype(F32)


def sds(shape, dtype):
    return jax.ShapeDtypeStruct(shape, dtype)


def vmem(*shape, dtype=F32):
    return pltpu.VMEM(shape, dtype)


def dma(n):
    return pltpu.SemaphoreType.DMA((2, n))


def run_heads(*args):
    whole = pl.BlockSpec(memory_space=pltpu.VMEM)
    smem = pl.BlockSpec(memory_space=pltpu.SMEM)
    plane = (T, D)
    made = pl.pallas_call(
        heads_kernel,
        out_shape=(sds((CTX, 3, TOK, D), BF16), sds((TOK, D), F32), sds((TOK, D), F32), sds((32, TOK), F32),
                   sds((CTX, 8, D), F32)),
        in_specs=[whole] * 8 + [smem],
        out_specs=[whole] * 5,
        scratch_shapes=[
            vmem(CTX, 3, TOK, D, dtype=BF16), vmem(3, T, D, dtype=BF16), vmem(2, T, D, dtype=BF16),
            vmem(CTX, 8, TOK), vmem(8, T), vmem(T, T, dtype=BF16), vmem(T, D, dtype=BF16), vmem(8, T), vmem(*plane),
            vmem(NB, D, D), vmem(2, T, W, dtype=BF16), vmem(2, T, W, dtype=BF16), vmem(2, T, W, dtype=BF16),
            vmem(*plane), vmem(*plane), vmem(*plane),
            vmem(2, T, W, dtype=BF16), vmem(T, W, dtype=BF16), vmem(8, T), vmem(*plane),
            vmem(CTX, TOK), vmem(CTX, TOK), vmem(CTX, TOK), vmem(CTX, CTX, TOK), vmem(8, T), vmem(*plane),
            vmem(*plane), vmem(*plane), vmem(*plane), vmem(3, T, D, dtype=BF16),
            vmem(2, T, D, dtype=BF16), vmem(T, D, dtype=BF16), vmem(T, D, dtype=BF16), vmem(CTX, TOK, D, dtype=BF16),
            vmem(TOK, D), vmem(TOK, D), vmem(8 * NB, W), vmem(8 * NB, W), vmem(8, T), vmem(CTX, 8, TOK),
            vmem(8, D), vmem(4, 8, D), vmem(8, D), vmem(CTX, 8, D), vmem(CTX, 3, TOK, D, dtype=BF16),
            dma(CTX), dma(CTX), dma(CTX), dma(CTX), dma(1), dma(CTX), dma(NB), dma(CTX), dma(1), dma(CTX), dma(4),
            dma(CTX), dma(CTX),
        ],
        compiler_params=pltpu.CompilerParams(vmem_limit_bytes=60 * 2**20, collective_id=0, has_side_effects=True),
        name="heads",
    )(*args)
    return pl.pallas_call(
        place_kernel,
        out_shape=(sds((3, TOK, CTX, D), BF16), sds((TOK, D), F32), sds((TOK, D), F32), sds((32, TOK), F32),
                   sds((CTX, D), F32), sds((1, 32), F32), sds((1, 1), F32)),
        in_specs=[whole] * 5 + [smem],
        out_specs=[whole] * 7,
        name="place",
        compiler_params=pltpu.CompilerParams(vmem_limit_bytes=16 * 2**20),
    )(*made, args[-1])


def local(qkv, ssd_b, ssd_c, step_size, decay_rate, value_weight, returns, step_labels, lengths):
    dqkv, gb, gc, gs, gvalue, grate, loss = run_heads(
        qkv[:, 0], ssd_b[0], ssd_c[0], step_size[0].T, step_labels, returns, decay_rate[None],
        value_weight.reshape(CTX, D), lengths)
    return (loss.reshape(()), dqkv[:, None], gb[None], gc[None], gs.T[None], grate.reshape(-1), gvalue.reshape(-1))


def solution(mesh):
    in_specs = (
        P(None, "rollout", "context", "head", None), P("rollout", "context", None), P("rollout", "context", None),
        P("rollout", "context", "head"), P("head"), P("head"), P("rollout", None), P("rollout", "context"), P(),
    )
    out_specs = (
        P(), P(None, "rollout", "context", "head", None), P("rollout", "context", None),
        P("rollout", "context", None), P("rollout", "context", "head"), P("head"), P("head"),
    )
    return jax.shard_map(local, mesh=mesh, in_specs=in_specs, out_specs=out_specs, check_vma=False)
```

```python
import functools
import math

import jax
import jax.numpy as jnp
from jax import lax
from jax.experimental import pallas as pl
from jax.experimental.pallas import tpu as pltpu
from jax.sharding import PartitionSpec as P

NORM_EPS = 1e-05
HI = lax.Precision.HIGHEST
F32 = jnp.float32
BF16 = jnp.bfloat16
T = 2048
W = 256
NB = T // W
D = 128
SCALE = 1.0 / math.sqrt(128.0)
LOG2E = 1.4426950408889634


def dot_nn(a, b, precision=None):
    return lax.dot_general(a, b, (((1,), (0,)), ((), ())), precision=precision, preferred_element_type=F32)


def dot_nt(a, b, precision=None):
    return lax.dot_general(a, b, (((1,), (1,)), ((), ())), precision=precision, preferred_element_type=F32)


def dot_tn(a, b, precision=None):
    return lax.dot_general(a, b, (((0,), (0,)), ((), ())), precision=precision, preferred_element_type=F32)


def parts3(a):
    high = a.astype(BF16).astype(F32)
    mid = (a - high).astype(BF16).astype(F32)
    low = a - high - mid
    return jnp.concatenate([high, mid, low, jnp.zeros_like(a)], axis=0).astype(BF16)


def wide(a):
    high, low = parts(a)
    return jnp.concatenate([high, low], axis=1)


def fold(a):
    return a[:, :D] + a[:, D:]


def parts(a):
    high = a.astype(BF16)
    return high, (a - high.astype(F32)).astype(BF16)


def rows(i):
    return pl.ds(i * W, W)


def iota(shape, dim):
    return lax.broadcasted_iota(jnp.int32, shape, dim)


def head_select():
    return jnp.where(iota((8, D), 1) // 64 == iota((8, D), 0), 1.0, 0.0).astype(F32)


def head_mean():
    return jnp.where(iota((D, D), 0) // 64 == iota((D, D), 1) // 64, 1.0 / 64.0, 0.0).astype(F32)


def attention_forward(q, k, v, p, x, arrive):
    causal = iota((W, W), 0) >= iota((W, W), 1)
    c = SCALE * LOG2E
    for i in range(NB):
        arrive(i)
        qi = q[rows(i), :]
        diag = jnp.where(causal, dot_nt(qi, k[rows(i), :]) * c, -1e30)
        top = jnp.max(diag, axis=1, keepdims=True)
        if i:
            past = dot_nt(qi, k[: i * W, :]) * c
            top = jnp.maximum(top, jnp.max(past, axis=1, keepdims=True))
            past = jnp.exp2(past - top)
        diag = jnp.exp2(diag - top)
        total = jnp.sum(diag, axis=1, keepdims=True)
        if i:
            total = total + jnp.sum(past, axis=1, keepdims=True)
        inverse = 1.0 / total
        pd = (diag * inverse).astype(BF16)
        p[rows(i), rows(i)] = pd
        o = dot_nn(pd, v[rows(i), :])
        if i:
            pp = (past * inverse).astype(BF16)
            p[rows(i), : i * W] = pp
            o = o + dot_nn(pp, v[: i * W, :])
        x[rows(i), :] = o.astype(BF16)


def ssd_prepare(b, c, step, rate, cum_rows, cum_cols, mask, gmask, glow):
    upto = jnp.where(iota((W, W), 0) <= iota((W, W), 1), 1.0, 0.0).astype(BF16)
    causal = iota((W, W), 0) >= iota((W, W), 1)
    hsel = head_select()
    hsel4 = jnp.concatenate([hsel] * 4, axis=0).astype(BF16)
    la = jnp.concatenate([-(step[:, rows(i)] * rate) for i in range(NB)], axis=0)
    sums = dot_nn(parts3(la), upto)
    sums = sums[: 8 * NB] + sums[8 * NB : 16 * NB] + sums[16 * NB : 24 * NB]
    for i in range(NB):
        cr = sums[8 * i : 8 * i + 8]
        ce = dot_tn(parts3(cr), hsel4)
        cum_rows[:, rows(i)] = cr
        cum_cols[rows(i), :] = ce
        g = dot_nt(c[rows(i), :], b[rows(i), :])
        for h in range(2):
            gap = ce[:, 64 * h : 64 * h + 1] - cr[h : h + 1, :]
            m = jnp.exp(jnp.where(causal, gap, -1e30))
            high, low = parts(g * m)
            mask[h, rows(i), :] = m.astype(BF16)
            gmask[h, rows(i), :] = high
            glow[h, rows(i), :] = low


def ssd_forward(x, b, c, w1, cum_cols, state, gmask, glow, unit, normed, carried, value):
    hmean = head_mean().astype(BF16)
    first = iota((W, D), 1) < 64
    w8 = jnp.broadcast_to(w1, (8, D)).astype(BF16)
    st = jnp.zeros((D, D), F32)

    def mean(a):
        high, low = parts(a)
        return dot_nn(high, hmean) + dot_nn(low, hmean)

    for i in range(NB):
        ce = cum_cols[rows(i), :]
        end = ce[W - 1 : W, :]
        bi, ci, xi = b[rows(i), :], c[rows(i), :], x[rows(i), :]
        state[i] = st
        ca = jnp.exp(ce) * fold(dot_nn(ci, wide(st)))
        carried[rows(i), :] = ca
        y = ca
        for h in range(2):
            xh = jnp.where(first == (h == 0), xi, jnp.zeros_like(xi))
            y = y + dot_nn(gmask[h, rows(i), :], xh) + dot_nn(glow[h, rows(i), :], xh)
        st = jnp.exp(end) * st + fold(dot_tn(bi, wide(xi.astype(F32) * jnp.exp(end - ce))))
        r = lax.rsqrt(mean(y * y) + NORM_EPS)
        n = y * r
        unit[rows(i), :] = r * (w1 - n * mean(n * w1))
        normed[rows(i), :] = n
        high, low = parts(n)
        part = dot_nt(w8, high) + dot_nt(w8, low)
        value[2 * i : 2 * i + 1, :] = part[0:1, :D]
        value[2 * i + 1 : 2 * i + 2, :] = part[0:1, D:]


def ssd_pairs(x, b, cum_cols, state, mask, gmask, unit, carried, pairs, gate, across, dcp):
    hselb = head_select().astype(BF16)
    first = iota((W, D), 1) < 64
    for i in range(NB):
        xi, u = x[rows(i), :], unit[rows(i), :]
        dg, row = None, None
        for h in range(2):
            high, low = parts(jnp.where(first == (h == 0), u, 0.0))
            ux = dot_nt(high, xi) + dot_nt(low, xi)
            part = ux * mask[h, rows(i), :].astype(F32)
            dg = part if dg is None else dg + part
            pair = (ux * gmask[h, rows(i), :].astype(F32)).astype(BF16)
            pairs[h, rows(i), :] = pair
            pick = jnp.where(iota((8, W), 0) == h, 1.0, 0.0).astype(BF16)
            term = dot_nt(pick, pair)
            row = term if row is None else row + term
        dgb = dg.astype(BF16)
        gate[rows(i), :] = dgb
        high, low = parts(u * carried[rows(i), :])
        across[:, rows(i)] = row + dot_nt(hselb, high) + dot_nt(hselb, low)
        ue = (u * jnp.exp(cum_cols[rows(i), :])).astype(BF16)
        dcp[rows(i), :] = dot_nn(dgb, b[rows(i), :]) + dot_nt(ue, state[i].astype(BF16))


def ssd_back_step(i, lam, gv, err, ecol, x, b, c, cum_cols, state, gmask, unit, normed, pairs, gate, across, dcp,
                  dx, db, dc, sums, cross):
    hsel = head_select()
    first = iota((W, D), 1) < 64
    ce = cum_cols[rows(i), :]
    end = ce[W - 1 : W, :]
    expc, tail, decay = jnp.exp(ce), jnp.exp(end - ce), jnp.exp(end)
    bi, ci, xi = b[rows(i), :], c[rows(i), :], x[rows(i), :]
    ee, er = ecol[rows(i), :], err[:, rows(i)]
    dy = ee * unit[rows(i), :]
    bl = fold(dot_nn(bi, wide(lam)))
    xt = xi.astype(F32) * tail
    dxi = tail * bl
    col = None
    for h in range(2):
        gm = gmask[h, rows(i), :]
        dxi = dxi + fold(dot_tn(gm, wide(jnp.where(first == (h == 0), dy, 0.0))))
        eh = jnp.where(iota((8, W), 0) == h, er, 0.0)
        high = eh.astype(BF16).astype(F32)
        two = dot_nn(jnp.concatenate([high, eh - high], axis=0).astype(BF16), pairs[h, rows(i), :])
        two = two[:8] + two[8:]
        col = two if col is None else col + two
    dx[rows(i), :] = dxi
    st = state[i]
    dc[rows(i), :] = (ee * dcp[rows(i), :]).astype(BF16)
    db[rows(i), :] = (
        dot_tn(gate[rows(i), :], (ee * ci.astype(F32)).astype(BF16)) + dot_nt(xt.astype(BF16), lam.astype(BF16))
    ).astype(BF16)
    through = jnp.sum(hsel * (decay * jnp.sum(st * lam, axis=0, keepdims=True)), axis=1, keepdims=True)
    sums[8 * i : 8 * i + 8, :] = er * across[:, rows(i)] - col + jnp.where(iota((8, W), 1) == W - 1, through, 0.0)
    high, low = parts(xt * bl)
    hselb = hsel.astype(BF16)
    cross[8 * i : 8 * i + 8, :] = dot_nt(hselb, high) + dot_nt(hselb, low)
    gv = gv + jnp.sum((ee * normed[rows(i), :]).reshape(W // 8, 8, D), axis=0)
    lam = decay * lam + fold(dot_tn(ci, wide(dy * expc)))
    return lam, gv


def ssd_finish(step, rate, sums, cross, gstep):
    suffix = jnp.where(iota((W, W), 0) >= iota((W, W), 1), 1.0, 0.0).astype(BF16)
    prefix = jnp.where(iota((W, W), 0) < iota((W, W), 1), 1.0, 0.0).astype(BF16)
    g = dot_nn(parts3(sums[...]), suffix) + dot_nn(parts3(cross[...]), prefix)
    g = g[: 8 * NB] + g[8 * NB : 16 * NB] + g[16 * NB : 24 * NB]
    gr = jnp.zeros((8, W), F32)
    for i in range(NB):
        gi = g[8 * i : 8 * i + 8]
        gstep[:, rows(i)] = -(gi * rate)
        gr = gr - gi * step[:, rows(i)]
    return jnp.sum(gr, axis=1, keepdims=True)


def attention_back_step(i, q, k, v, p, x, dx, dk_acc, dv_acc, dqkv):
    n = (i + 1) * W
    do = dx[rows(i), :].astype(BF16)
    delta = jnp.sum(do.astype(F32) * x[rows(i), :].astype(F32), axis=1, keepdims=True)
    pi = p[rows(i), :n]
    qi = q[rows(i), :]
    ds = (pi.astype(F32) * (dot_nt(do, v[:n, :]) - delta)).astype(BF16)
    dqkv[0, rows(i), :] = (dot_nn(ds, k[:n, :]) * SCALE).astype(BF16)
    dk = dot_tn(ds, qi)
    dv = dot_tn(pi, do)
    if i < NB - 1:
        dk = dk + dk_acc[:n, :]
        dv = dv + dv_acc[:n, :]
    if i:
        dk_acc[: n - W, :] = dk[: n - W]
        dv_acc[: n - W, :] = dv[: n - W]
    dqkv[1, rows(i), :] = (dk[n - W :] * SCALE).astype(BF16)
    dqkv[2, rows(i), :] = dv[n - W :].astype(BF16)


MESH = pl.DeviceIdType.MESH
GROUP = 8
CTX = 16
TOK = 128


def put(src, dst, sems, slot_out, slot_in, **where):
    return pltpu.make_async_remote_copy(
        src_ref=src, dst_ref=dst, send_sem=sems.at[0, slot_out], recv_sem=sems.at[1, slot_in],
        device_id=where, device_id_type=MESH,
    )


def block(i):
    return pl.ds(pl.multiple_of(i * TOK, TOK), TOK)


def others(me, act):
    def body(o, carry):
        act(lax.rem(me + o, CTX))
        return carry

    lax.fori_loop(1, CTX, body, 0)


def heads_kernel(qkv_in, b_in, c_in, step_in, labels, table, rate_in, weight_in, lengths,
                 land_out, rest_out,
                 stage, qkv, bc, aux_out, aux, p, x, cum_rows, cum_cols, state, mask, gmask, glow, unit, normed, carried,
                 pairs, gate, across, dcp, vpart, vpair, vchip, vall, err, ecol, dx, dk_acc, dv_acc, dqkv,
                 dbc, dpair, dsum, dall, gres, gother, sums, cross, gstep, gs_in, small, small_x, small_sum, small_all,
                 land, s_qkv, s_bc, s_twin, s_aux, s_vp, s_v, s_dp, s_d, s_g, s_gs, s_x, s_sm, s_out):
    me = lax.axis_index("context")
    core = lax.axis_index("head")
    rollout = lax.axis_index("rollout")
    twin = 1 - core
    barrier = pltpu.get_barrier_semaphore()
    others(me, lambda d: pl.semaphore_signal(barrier, inc=1, device_id={"context": d}, device_id_type=MESH))
    pl.semaphore_signal(barrier, inc=1, device_id={"head": twin}, device_id_type=MESH)
    for o in range(1, 4):
        pl.semaphore_signal(barrier, inc=1, device_id={"rollout": lax.rem(rollout + o, 4)}, device_id_type=MESH)

    onehot = jnp.where(iota((64, TOK), 0) == labels[...], 1.0, 0.0).astype(F32)
    target = dot_nn(jnp.broadcast_to(table[...], (8, 64)), onehot, HI)[0:1]
    for d in range(CTX):
        aux_out[d] = jnp.concatenate([step_in[2 * d : 2 * d + 2, :], target, jnp.zeros((5, TOK), F32)], axis=0)
    bc[0, block(me)] = b_in[...]
    bc[1, block(me)] = c_in[...]
    pl.semaphore_wait(barrier, CTX + 3)

    def send_aux(d):
        return put(aux_out.at[d], aux.at[:, block(me)], s_aux, d, me, context=d)

    def send_bc(d):
        return put(bc.at[core, block(me)], bc.at[core, block(me)], s_bc, d, me, context=d)

    def send_qkv(d):
        return put(stage.at[d], qkv.at[:, block(me)], s_qkv, d, me, context=d)

    def send_early(d):
        send_bc(d).start()
        send_aux(d).start()

    others(me, send_early)
    for i in range(3):
        stage[:, i] = jnp.swapaxes(qkv_in[i], 0, 1)
    others(me, lambda d: send_qkv(d).start())
    qkv[:, block(me)] = stage[me]
    aux[:, block(me)] = aux_out[me]
    rate = jnp.sum(
        jnp.where((iota((8, 32), 1) == 2 * me + iota((8, 32), 0)) & (iota((8, 32), 0) < 2), rate_in[...], 0.0),
        axis=1, keepdims=True,
    )
    w1 = jnp.sum(jnp.where(iota((CTX, D), 0) == me, weight_in[...].astype(F32), 0.0), axis=0, keepdims=True)

    def got_bc(s):
        put(bc.at[core, block(s)], bc.at[core, block(s)], s_bc, s, s, context=s).wait_recv()

    others(me, got_bc)

    def send_twin(s):
        return put(bc.at[core, block(s)], bc.at[core, block(s)], s_twin, s, s, head=twin)

    others(me, lambda s: send_twin(s).start())
    others(me, lambda s: put(aux_out.at[s], aux.at[:, block(s)], s_aux, s, s, context=s).wait_recv())
    others(me, lambda s: put(bc.at[twin, block(s)], bc.at[twin, block(s)], s_twin, s, s, head=twin).wait_recv())
    b, c = bc.at[0], bc.at[1]
    ssd_prepare(b, c, aux, rate, cum_rows, cum_cols, mask, gmask, glow)

    def arrive(i):
        for s in (2 * i, 2 * i + 1):
            @pl.when(me != s)
            def _():
                put(stage.at[s], qkv.at[:, block(s)], s_qkv, s, s, context=s).wait_recv()

    attention_forward(qkv.at[0], qkv.at[1], qkv.at[2], p, x, arrive)
    ssd_forward(x, b, c, w1, cum_cols, state, gmask, glow, unit, normed, carried, vpart)

    pair = put(vpart, vpair, s_vp, 0, 0, head=twin)
    pair.start()
    pair.wait_recv()
    vchip[...] = vpart[...] + vpair[...]
    vall[me] = vchip[...]
    others(me, lambda d: put(vchip, vall.at[me], s_v, d, me, context=d).start())
    ssd_pairs(x, b, cum_cols, state, mask, gmask, unit, carried, pairs, gate, across, dcp)
    others(me, lambda s: put(vchip, vall.at[s], s_v, s, s, context=s).wait_recv())
    value = vall[0]
    for s in range(1, CTX):
        value = value + vall[s]
    limit = lengths[rollout]
    loss = jnp.zeros((1, TOK), F32)
    for s in range(CTX):
        valid = jnp.where(iota((1, TOK), 1) + s * TOK < limit, 1.0, 0.0).astype(F32)
        e = (value[s : s + 1] - aux[2:3, s * TOK : (s + 1) * TOK]) * valid
        loss = loss + e * e
        err[:, s * TOK : (s + 1) * TOK] = jnp.broadcast_to(e, (8, TOK))
    row0 = jnp.where(iota((8, D), 0) == 0, 1.0, 0.0).astype(F32)
    ecol[...] = dot_tn(parts3(err[...]), jnp.concatenate([row0] * 4, axis=0).astype(BF16))

    half = T // 2

    def send_pair(i):
        part = pl.ds(i * half, half)
        return put(dbc.at[twin, part], dpair.at[part], s_dp, i, i, head=twin)

    lam = jnp.zeros((D, D), F32)
    gv = jnp.zeros((8, D), F32)
    for i in reversed(range(NB)):
        lam, gv = ssd_back_step(i, lam, gv, err, ecol, x, b, c, cum_cols, state, gmask, unit, normed, pairs, gate,
                                across, dcp, dx, dbc.at[0], dbc.at[1], sums, cross)
        if i % (NB // 2) == 0:
            send_pair(i // (NB // 2)).start()
    gr = ssd_finish(aux, rate, sums, cross, gstep)
    small[...] = jnp.concatenate(
        [jnp.sum(gv, axis=0, keepdims=True), jnp.broadcast_to(gr[0:1], (1, D)), jnp.broadcast_to(gr[1:2], (1, D)),
         jnp.broadcast_to(0.5 * jnp.sum(loss, axis=1, keepdims=True), (1, D)), jnp.zeros((4, D), F32)], axis=0)
    small_x[rollout] = small[...]

    def send_x(o):
        d = lax.rem(rollout + o, 4)
        return put(small, small_x.at[rollout], s_x, d, rollout, rollout=d)

    def send_gs(d):
        return put(gstep.at[:, block(d)], gs_in.at[me], s_gs, d, me, context=d)

    def send_small(d):
        return put(small_sum, small_all.at[me], s_sm, d, me, context=d)

    def send_d(d):
        return put(dsum.at[block(d)], dall.at[me], s_d, d, me, context=d)

    def send_out(d):
        return put(dqkv.at[:, block(d)], land.at[me], s_out, d, me, context=d)

    for o in range(1, 4):
        send_x(o).start()
    q, k, v = qkv.at[0], qkv.at[1], qkv.at[2]
    for i in reversed(range(NB)):
        attention_back_step(i, q, k, v, p, x, dx, dk_acc, dv_acc, dqkv)
        if i == NB - 1:
            send_pair(0).wait_recv()
            send_pair(1).wait_recv()
            dsum[...] = (dbc[core].astype(F32) + dpair[...].astype(F32)).astype(BF16)
            others(me, lambda d: send_d(d).start())
            dall[me] = dsum[block(me)]
            others(me, lambda d: send_gs(d).start())
            gs_in[me] = gstep[:, block(me)]
        if i == NB - 2:
            for o in range(1, 4):
                d = lax.rem(rollout + o, 4)
                put(small, small_x.at[d], s_x, d, d, rollout=d).wait_recv()
            small_sum[...] = (small_x[0] + small_x[1]) + (small_x[2] + small_x[3])
            others(me, lambda d: send_small(d).start())
            small_all[me] = small_sum[...]
        if i % GROUP == 0:
            def send_group(o, carry):
                d = 2 * i + lax.rem(me + o, 2 * GROUP)

                @pl.when(me != d)
                def _():
                    send_out(d).start()

                return carry

            lax.fori_loop(0, 2 * GROUP, send_group, 0)
    land[me] = dqkv[:, block(me)]

    others(me, lambda s: put(dsum.at[block(s)], dall.at[s], s_d, s, s, context=s).wait_recv())
    total = dall[0].astype(F32)
    for s in range(1, CTX):
        total = total + dall[s].astype(F32)
    gres[...] = total
    swap = put(gres, gother, s_g, 0, 0, head=twin)
    swap.start()
    others(me, lambda s: put(gstep.at[:, block(s)], gs_in.at[s], s_gs, s, s, context=s).wait_recv())
    rest_out[256:288, :] = jnp.concatenate([gs_in[s, 0:2] for s in range(CTX)], axis=0)
    others(me, lambda s: put(small_sum, small_all.at[s], s_sm, s, s, context=s).wait_recv())
    rest_out[288:, :] = jnp.concatenate([small_all[s] for s in range(CTX)], axis=0)
    swap.wait_recv()
    mine, other = gres[...], gother[...]
    rest_out[0:128, :] = jnp.where(core == 0, mine, other)
    rest_out[128:256, :] = jnp.where(core == 0, other, mine)
    others(me, lambda s: put(dqkv.at[:, block(s)], land.at[s], s_out, s, s, context=s).wait_recv())
    land_out[...] = land[...]

    def sent(d):
        send_qkv(d).wait_send()
        send_aux(d).wait_send()
        send_bc(d).wait_send()
        send_twin(d).wait_send()
        put(vchip, vall.at[me], s_v, d, me, context=d).wait_send()
        send_gs(d).wait_send()
        send_d(d).wait_send()
        send_small(d).wait_send()
        send_out(d).wait_send()

    others(me, sent)
    for o in range(1, 4):
        send_x(o).wait_send()
    for i in range(2):
        send_pair(i).wait_send()
    pair.wait_send()
    swap.wait_send()


def place_kernel(land_in, rest_in, lengths, dqkv_out, gb_out, gc_out, gs_out, gvalue_out, grate_out, loss_out,
                 land, rest, sem):
    copies = [pltpu.make_async_copy(land_in.at[:, i], land.at[i], sem.at[i]) for i in range(3)]
    copies.append(pltpu.make_async_copy(rest_in, rest, sem.at[3]))
    for copy in copies:
        copy.start()
    copies[3].wait()
    gb_out[...] = rest[0:128, :]
    gc_out[...] = rest[128:256, :]
    gs_out[...] = rest[256:288, :]
    lane = iota((1, 32), 1)
    grate = jnp.zeros((1, 32), F32)
    for s in range(CTX):
        gvalue_out[s : s + 1, :] = rest[288 + 8 * s : 289 + 8 * s, :]
        for h in range(2):
            row = 289 + 8 * s + h
            grate = jnp.where(lane == 2 * s + h, rest[row : row + 1, 0:32], grate)
    grate_out[...] = grate
    count = lengths[0] + lengths[1] + lengths[2] + lengths[3]
    loss_out[...] = rest[291:292, 0:1] / jnp.full((1, 1), count, jnp.int32).astype(F32)
    for i in range(3):
        copies[i].wait()
        dqkv_out[i] = jnp.swapaxes(land[i], 0, 1)


def sds(shape, dtype):
    return jax.ShapeDtypeStruct(shape, dtype)


def vmem(*shape, dtype=F32):
    return pltpu.VMEM(shape, dtype)


def dma(n):
    return pltpu.SemaphoreType.DMA((2, n))


def run_heads(*args):
    whole = pl.BlockSpec(memory_space=pltpu.VMEM)
    smem = pl.BlockSpec(memory_space=pltpu.SMEM)
    plane = (T, D)
    made = pl.pallas_call(
        heads_kernel,
        out_shape=(sds((CTX, 3, TOK, D), BF16), sds((416, D), F32)),
        in_specs=[whole] * 8 + [smem],
        out_specs=[whole] * 2,
        scratch_shapes=[
            vmem(CTX, 3, TOK, D, dtype=BF16), vmem(3, T, D, dtype=BF16), vmem(2, T, D, dtype=BF16),
            vmem(CTX, 8, TOK), vmem(8, T), vmem(T, T, dtype=BF16), vmem(T, D, dtype=BF16), vmem(8, T), vmem(*plane),
            vmem(NB, D, D), vmem(2, T, W, dtype=BF16), vmem(2, T, W, dtype=BF16), vmem(2, T, W, dtype=BF16),
            vmem(*plane), vmem(*plane), vmem(*plane),
            vmem(2, T, W, dtype=BF16), vmem(T, W, dtype=BF16), vmem(8, T), vmem(*plane),
            vmem(CTX, TOK), vmem(CTX, TOK), vmem(CTX, TOK), vmem(CTX, CTX, TOK), vmem(8, T), vmem(*plane),
            vmem(*plane), vmem(*plane), vmem(*plane), vmem(3, T, D, dtype=BF16),
            vmem(2, T, D, dtype=BF16), vmem(T, D, dtype=BF16), vmem(T, D, dtype=BF16), vmem(CTX, TOK, D, dtype=BF16),
            vmem(TOK, D), vmem(TOK, D), vmem(8 * NB, W), vmem(8 * NB, W), vmem(8, T), vmem(CTX, 8, TOK),
            vmem(8, D), vmem(4, 8, D), vmem(8, D), vmem(CTX, 8, D), vmem(CTX, 3, TOK, D, dtype=BF16),
            dma(CTX), dma(CTX), dma(CTX), dma(CTX), dma(1), dma(CTX), dma(2), dma(CTX), dma(1), dma(CTX), dma(4),
            dma(CTX), dma(CTX),
        ],
        compiler_params=pltpu.CompilerParams(vmem_limit_bytes=60 * 2**20, collective_id=0, has_side_effects=True),
        name="heads",
    )(*args)
    return pl.pallas_call(
        place_kernel,
        out_shape=(sds((3, TOK, CTX, D), BF16), sds((TOK, D), F32), sds((TOK, D), F32), sds((32, TOK), F32),
                   sds((CTX, D), F32), sds((1, 32), F32), sds((1, 1), F32)),
        in_specs=[pl.BlockSpec(memory_space=pl.ANY)] * 2 + [smem],
        out_specs=[whole] * 7,
        scratch_shapes=[vmem(3, CTX, TOK, D, dtype=BF16), vmem(416, D), pltpu.SemaphoreType.DMA((4,))],
        name="place",
        compiler_params=pltpu.CompilerParams(vmem_limit_bytes=60 * 2**20),
    )(*made, args[-1])


def local(qkv, ssd_b, ssd_c, step_size, decay_rate, value_weight, returns, step_labels, lengths):
    dqkv, gb, gc, gs, gvalue, grate, loss = run_heads(
        qkv[:, 0], ssd_b[0], ssd_c[0], step_size[0].T, step_labels, returns, decay_rate[None],
        value_weight.reshape(CTX, D), lengths)
    return (loss.reshape(()), dqkv[:, None], gb[None], gc[None], gs.T[None], grate.reshape(-1), gvalue.reshape(-1))


def solution(mesh):
    in_specs = (
        P(None, "rollout", "context", "head", None), P("rollout", "context", None), P("rollout", "context", None),
        P("rollout", "context", "head"), P("head"), P("head"), P("rollout", None), P("rollout", "context"), P(),
    )
    out_specs = (
        P(), P(None, "rollout", "context", "head", None), P("rollout", "context", None),
        P("rollout", "context", None), P("rollout", "context", "head"), P("head"), P("head"),
    )
    return jax.shard_map(local, mesh=mesh, in_specs=in_specs, out_specs=out_specs, check_vma=False)
```

```python
import functools
import math

import jax
import jax.numpy as jnp
from jax import lax
from jax.experimental import pallas as pl
from jax.experimental.pallas import tpu as pltpu
from jax.sharding import PartitionSpec as P

NORM_EPS = 1e-05
HI = lax.Precision.HIGHEST
F32 = jnp.float32
BF16 = jnp.bfloat16
T = 2048
W = 256
NB = T // W
D = 128
SCALE = 1.0 / math.sqrt(128.0)
LOG2E = 1.4426950408889634


def dot_nn(a, b, precision=None):
    return lax.dot_general(a, b, (((1,), (0,)), ((), ())), precision=precision, preferred_element_type=F32)


def dot_nt(a, b, precision=None):
    return lax.dot_general(a, b, (((1,), (1,)), ((), ())), precision=precision, preferred_element_type=F32)


def dot_tn(a, b, precision=None):
    return lax.dot_general(a, b, (((0,), (0,)), ((), ())), precision=precision, preferred_element_type=F32)


def parts3(a):
    high = a.astype(BF16).astype(F32)
    mid = (a - high).astype(BF16).astype(F32)
    low = a - high - mid
    return jnp.concatenate([high, mid, low, jnp.zeros_like(a)], axis=0).astype(BF16)


def wide(a):
    high, low = parts(a)
    return jnp.concatenate([high, low], axis=1)


def fold(a):
    return a[:, :D] + a[:, D:]


def parts(a):
    high = a.astype(BF16)
    return high, (a - high.astype(F32)).astype(BF16)


def rows(i):
    return pl.ds(i * W, W)


def iota(shape, dim):
    return lax.broadcasted_iota(jnp.int32, shape, dim)


def head_select():
    return jnp.where(iota((8, D), 1) // 64 == iota((8, D), 0), 1.0, 0.0).astype(F32)


def head_mean():
    return jnp.where(iota((D, D), 0) // 64 == iota((D, D), 1) // 64, 1.0 / 64.0, 0.0).astype(F32)


def attention_probs(q, k, p, arrive):
    causal = iota((W, W), 0) >= iota((W, W), 1)
    c = SCALE * LOG2E
    for i in range(NB):
        arrive(i)
        qi = q[rows(i), :]
        diag = jnp.where(causal, dot_nt(qi, k[rows(i), :]) * c, -1e30)
        top = jnp.max(diag, axis=1, keepdims=True)
        if i:
            past = dot_nt(qi, k[: i * W, :]) * c
            top = jnp.maximum(top, jnp.max(past, axis=1, keepdims=True))
            past = jnp.exp2(past - top)
        diag = jnp.exp2(diag - top)
        total = jnp.sum(diag, axis=1, keepdims=True)
        if i:
            total = total + jnp.sum(past, axis=1, keepdims=True)
        inverse = 1.0 / total
        p[rows(i), rows(i)] = (diag * inverse).astype(BF16)
        if i:
            p[rows(i), : i * W] = (past * inverse).astype(BF16)


def attention_mix(p, v, x, arrive):
    for i in range(NB):
        arrive(i)
        n = (i + 1) * W
        x[rows(i), :] = dot_nn(p[rows(i), :n], v[:n, :]).astype(BF16)


def ssd_prepare(b, c, step, rate, cum_rows, cum_cols, mask, gmask, glow):
    upto = jnp.where(iota((W, W), 0) <= iota((W, W), 1), 1.0, 0.0).astype(BF16)
    causal = iota((W, W), 0) >= iota((W, W), 1)
    hsel = head_select()
    hsel4 = jnp.concatenate([hsel] * 4, axis=0).astype(BF16)
    la = jnp.concatenate([-(step[:, rows(i)] * rate) for i in range(NB)], axis=0)
    sums = dot_nn(parts3(la), upto)
    sums = sums[: 8 * NB] + sums[8 * NB : 16 * NB] + sums[16 * NB : 24 * NB]
    for i in range(NB):
        cr = sums[8 * i : 8 * i + 8]
        ce = dot_tn(parts3(cr), hsel4)
        cum_rows[:, rows(i)] = cr
        cum_cols[rows(i), :] = ce
        g = dot_nt(c[rows(i), :], b[rows(i), :])
        for h in range(2):
            gap = ce[:, 64 * h : 64 * h + 1] - cr[h : h + 1, :]
            m = jnp.exp(jnp.where(causal, gap, -1e30))
            high, low = parts(g * m)
            mask[h, rows(i), :] = m.astype(BF16)
            gmask[h, rows(i), :] = high
            glow[h, rows(i), :] = low


def ssd_forward(x, b, c, w1, cum_cols, state, gmask, glow, unit, normed, carried, value):
    hmean = head_mean().astype(BF16)
    first = iota((W, D), 1) < 64
    w8 = jnp.broadcast_to(w1, (8, D)).astype(BF16)
    st = jnp.zeros((D, D), F32)

    def mean(a):
        high, low = parts(a)
        return dot_nn(high, hmean) + dot_nn(low, hmean)

    for i in range(NB):
        ce = cum_cols[rows(i), :]
        end = ce[W - 1 : W, :]
        bi, ci, xi = b[rows(i), :], c[rows(i), :], x[rows(i), :]
        state[i] = st
        ca = jnp.exp(ce) * fold(dot_nn(ci, wide(st)))
        carried[rows(i), :] = ca
        y = ca
        for h in range(2):
            xh = jnp.where(first == (h == 0), xi, jnp.zeros_like(xi))
            y = y + dot_nn(gmask[h, rows(i), :], xh) + dot_nn(glow[h, rows(i), :], xh)
        st = jnp.exp(end) * st + fold(dot_tn(bi, wide(xi.astype(F32) * jnp.exp(end - ce))))
        r = lax.rsqrt(mean(y * y) + NORM_EPS)
        n = y * r
        unit[rows(i), :] = r * (w1 - n * mean(n * w1))
        normed[rows(i), :] = n
        high, low = parts(n)
        part = dot_nt(w8, high) + dot_nt(w8, low)
        value[2 * i : 2 * i + 1, :] = part[0:1, :D]
        value[2 * i + 1 : 2 * i + 2, :] = part[0:1, D:]


def ssd_pairs(x, b, cum_cols, state, mask, gmask, unit, carried, pairs, gate, across, dcp):
    hselb = head_select().astype(BF16)
    first = iota((W, D), 1) < 64
    for i in range(NB):
        xi, u = x[rows(i), :], unit[rows(i), :]
        dg, row = None, None
        for h in range(2):
            high, low = parts(jnp.where(first == (h == 0), u, 0.0))
            ux = dot_nt(high, xi) + dot_nt(low, xi)
            part = ux * mask[h, rows(i), :].astype(F32)
            dg = part if dg is None else dg + part
            pair = (ux * gmask[h, rows(i), :].astype(F32)).astype(BF16)
            pairs[h, rows(i), :] = pair
            pick = jnp.where(iota((8, W), 0) == h, 1.0, 0.0).astype(BF16)
            term = dot_nt(pick, pair)
            row = term if row is None else row + term
        dgb = dg.astype(BF16)
        gate[rows(i), :] = dgb
        high, low = parts(u * carried[rows(i), :])
        across[:, rows(i)] = row + dot_nt(hselb, high) + dot_nt(hselb, low)
        ue = (u * jnp.exp(cum_cols[rows(i), :])).astype(BF16)
        dcp[rows(i), :] = dot_nn(dgb, b[rows(i), :]) + dot_nt(ue, state[i].astype(BF16))


def ssd_back_step(i, lam, gv, err, ecol, x, b, c, cum_cols, state, gmask, unit, normed, pairs, gate, across, dcp,
                  dx, db, dc, sums, cross):
    hsel = head_select()
    first = iota((W, D), 1) < 64
    ce = cum_cols[rows(i), :]
    end = ce[W - 1 : W, :]
    expc, tail, decay = jnp.exp(ce), jnp.exp(end - ce), jnp.exp(end)
    bi, ci, xi = b[rows(i), :], c[rows(i), :], x[rows(i), :]
    ee, er = ecol[rows(i), :], err[:, rows(i)]
    dy = ee * unit[rows(i), :]
    bl = fold(dot_nn(bi, wide(lam)))
    xt = xi.astype(F32) * tail
    dxi = tail * bl
    col = None
    for h in range(2):
        gm = gmask[h, rows(i), :]
        dxi = dxi + fold(dot_tn(gm, wide(jnp.where(first == (h == 0), dy, 0.0))))
        eh = jnp.where(iota((8, W), 0) == h, er, 0.0)
        high = eh.astype(BF16).astype(F32)
        two = dot_nn(jnp.concatenate([high, eh - high], axis=0).astype(BF16), pairs[h, rows(i), :])
        two = two[:8] + two[8:]
        col = two if col is None else col + two
    dx[rows(i), :] = dxi
    st = state[i]
    dc[rows(i), :] = (ee * dcp[rows(i), :]).astype(BF16)
    db[rows(i), :] = (
        dot_tn(gate[rows(i), :], (ee * ci.astype(F32)).astype(BF16)) + dot_nt(xt.astype(BF16), lam.astype(BF16))
    ).astype(BF16)
    through = jnp.sum(hsel * (decay * jnp.sum(st * lam, axis=0, keepdims=True)), axis=1, keepdims=True)
    sums[8 * i : 8 * i + 8, :] = er * across[:, rows(i)] - col + jnp.where(iota((8, W), 1) == W - 1, through, 0.0)
    high, low = parts(xt * bl)
    hselb = hsel.astype(BF16)
    cross[8 * i : 8 * i + 8, :] = dot_nt(hselb, high) + dot_nt(hselb, low)
    gv = gv + jnp.sum((ee * normed[rows(i), :]).reshape(W // 8, 8, D), axis=0)
    lam = decay * lam + fold(dot_tn(ci, wide(dy * expc)))
    return lam, gv


def ssd_finish(step, rate, sums, cross, gstep):
    suffix = jnp.where(iota((W, W), 0) >= iota((W, W), 1), 1.0, 0.0).astype(BF16)
    prefix = jnp.where(iota((W, W), 0) < iota((W, W), 1), 1.0, 0.0).astype(BF16)
    g = dot_nn(parts3(sums[...]), suffix) + dot_nn(parts3(cross[...]), prefix)
    g = g[: 8 * NB] + g[8 * NB : 16 * NB] + g[16 * NB : 24 * NB]
    gr = jnp.zeros((8, W), F32)
    for i in range(NB):
        gi = g[8 * i : 8 * i + 8]
        gstep[:, rows(i)] = -(gi * rate)
        gr = gr - gi * step[:, rows(i)]
    return jnp.sum(gr, axis=1, keepdims=True)


def value_back_step(i, p, dx, dop, dqkv):
    dop[rows(i), :] = dx[rows(i), :].astype(BF16)
    dqkv[2, rows(i), :] = dot_tn(p[i * W :, rows(i)], dop[i * W :, :]).astype(BF16)


def attention_back_step(i, q, k, v, p, x, dop, dk_acc, dqkv):
    n = (i + 1) * W
    do = dop[rows(i), :]
    delta = jnp.sum(do.astype(F32) * x[rows(i), :].astype(F32), axis=1, keepdims=True)
    ds = (p[rows(i), :n].astype(F32) * (dot_nt(do, v[:n, :]) - delta)).astype(BF16)
    dqkv[0, rows(i), :] = (dot_nn(ds, k[:n, :]) * SCALE).astype(BF16)
    dk = dot_tn(ds, q[rows(i), :])
    if i < NB - 1:
        dk = dk + dk_acc[:n, :]
    if i:
        dk_acc[: n - W, :] = dk[: n - W]
    dqkv[1, rows(i), :] = (dk[n - W :] * SCALE).astype(BF16)


MESH = pl.DeviceIdType.MESH
CTX = 16
TOK = 128


def put(src, dst, sems, slot_out, slot_in, **where):
    return pltpu.make_async_remote_copy(
        src_ref=src, dst_ref=dst, send_sem=sems.at[0, slot_out], recv_sem=sems.at[1, slot_in],
        device_id=where, device_id_type=MESH,
    )


def block(i):
    return pl.ds(pl.multiple_of(i * TOK, TOK), TOK)


def others(me, act):
    def body(o, carry):
        act(lax.rem(me + o, CTX))
        return carry

    lax.fori_loop(1, CTX, body, 0)


def heads_kernel(qkv_in, b_in, c_in, step_in, labels, table, rate_in, weight_in, lengths,
                 land_out, rest_out,
                 stage, qkv, bc, aux_out, aux, p, x, cum_rows, cum_cols, state, mask, gmask, glow, unit, normed, carried,
                 pairs, gate, across, dcp, vpart, vpair, vchip, vall, err, ecol, dx, dk_acc, dop, dqkv,
                 dbc, dpair, dsum, dall, gres, gother, sums, cross, gstep, gs_in, small, small_x, small_sum, small_all,
                 land, s_qkv, s_bc, s_twin, s_aux, s_vp, s_v, s_dp, s_d, s_g, s_gs, s_x, s_sm, s_out, s_qkv2, s_out2):
    me = lax.axis_index("context")
    core = lax.axis_index("head")
    rollout = lax.axis_index("rollout")
    twin = 1 - core
    barrier = pltpu.get_barrier_semaphore()
    others(me, lambda d: pl.semaphore_signal(barrier, inc=1, device_id={"context": d}, device_id_type=MESH))
    pl.semaphore_signal(barrier, inc=1, device_id={"head": twin}, device_id_type=MESH)
    for o in range(1, 4):
        pl.semaphore_signal(barrier, inc=1, device_id={"rollout": lax.rem(rollout + o, 4)}, device_id_type=MESH)

    onehot = jnp.where(iota((64, TOK), 0) == labels[...], 1.0, 0.0).astype(F32)
    target = dot_nn(jnp.broadcast_to(table[...], (8, 64)), onehot, HI)[0:1]
    for d in range(CTX):
        aux_out[d] = jnp.concatenate([step_in[2 * d : 2 * d + 2, :], target, jnp.zeros((5, TOK), F32)], axis=0)
    bc[0, block(me)] = b_in[...]
    bc[1, block(me)] = c_in[...]
    pl.semaphore_wait(barrier, CTX + 3)

    def send_aux(d):
        return put(aux_out.at[d], aux.at[:, block(me)], s_aux, d, me, context=d)

    def send_bc(d):
        return put(bc.at[core, block(me)], bc.at[core, block(me)], s_bc, d, me, context=d)

    def send_qkv(d):
        return put(stage.at[d, pl.ds(0, 2)], qkv.at[pl.ds(0, 2), block(me)], s_qkv, d, me, context=d)

    def send_v(d):
        return put(stage.at[d, 2], qkv.at[2, block(me)], s_qkv2, d, me, context=d)

    def send_early(d):
        send_aux(d).start()

    others(me, send_early)
    for i in range(3):
        stage[:, i] = jnp.swapaxes(qkv_in[i], 0, 1)
    others(me, lambda d: send_qkv(d).start())
    others(me, lambda d: send_bc(d).start())
    others(me, lambda d: send_v(d).start())
    qkv[:, block(me)] = stage[me]
    aux[:, block(me)] = aux_out[me]
    rate = jnp.sum(
        jnp.where((iota((8, 32), 1) == 2 * me + iota((8, 32), 0)) & (iota((8, 32), 0) < 2), rate_in[...], 0.0),
        axis=1, keepdims=True,
    )
    w1 = jnp.sum(jnp.where(iota((CTX, D), 0) == me, weight_in[...].astype(F32), 0.0), axis=0, keepdims=True)

    def arrive(i):
        for s in (2 * i, 2 * i + 1):
            @pl.when(me != s)
            def _():
                put(stage.at[s, pl.ds(0, 2)], qkv.at[pl.ds(0, 2), block(s)], s_qkv, s, s, context=s).wait_recv()

    def arrive_v(i):
        for s in (2 * i, 2 * i + 1):
            @pl.when(me != s)
            def _():
                put(stage.at[s, 2], qkv.at[2, block(s)], s_qkv2, s, s, context=s).wait_recv()

    attention_probs(qkv.at[0], qkv.at[1], p, arrive)
    def got_bc(s):
        put(bc.at[core, block(s)], bc.at[core, block(s)], s_bc, s, s, context=s).wait_recv()

    others(me, got_bc)

    def send_twin(s):
        return put(bc.at[core, block(s)], bc.at[core, block(s)], s_twin, s, s, head=twin)

    others(me, lambda s: send_twin(s).start())
    attention_mix(p, qkv.at[2], x, arrive_v)
    others(me, lambda s: put(aux_out.at[s], aux.at[:, block(s)], s_aux, s, s, context=s).wait_recv())
    others(me, lambda s: put(bc.at[twin, block(s)], bc.at[twin, block(s)], s_twin, s, s, head=twin).wait_recv())
    b, c = bc.at[0], bc.at[1]
    ssd_prepare(b, c, aux, rate, cum_rows, cum_cols, mask, gmask, glow)

    ssd_forward(x, b, c, w1, cum_cols, state, gmask, glow, unit, normed, carried, vpart)

    pair = put(vpart, vpair, s_vp, 0, 0, head=twin)
    pair.start()
    pair.wait_recv()
    vchip[...] = vpart[...] + vpair[...]
    vall[me] = vchip[...]
    others(me, lambda d: put(vchip, vall.at[me], s_v, d, me, context=d).start())
    ssd_pairs(x, b, cum_cols, state, mask, gmask, unit, carried, pairs, gate, across, dcp)
    others(me, lambda s: put(vchip, vall.at[s], s_v, s, s, context=s).wait_recv())
    value = vall[0]
    for s in range(1, CTX):
        value = value + vall[s]
    limit = lengths[rollout]
    loss = jnp.zeros((1, TOK), F32)
    for s in range(CTX):
        valid = jnp.where(iota((1, TOK), 1) + s * TOK < limit, 1.0, 0.0).astype(F32)
        e = (value[s : s + 1] - aux[2:3, s * TOK : (s + 1) * TOK]) * valid
        loss = loss + e * e
        err[:, s * TOK : (s + 1) * TOK] = jnp.broadcast_to(e, (8, TOK))
    row0 = jnp.where(iota((8, D), 0) == 0, 1.0, 0.0).astype(F32)
    ecol[...] = dot_tn(parts3(err[...]), jnp.concatenate([row0] * 4, axis=0).astype(BF16))

    half = T // 2

    def send_pair(i):
        part = pl.ds(i * half, half)
        return put(dbc.at[twin, part], dpair.at[part], s_dp, i, i, head=twin)

    lam = jnp.zeros((D, D), F32)
    gv = jnp.zeros((8, D), F32)
    for i in reversed(range(NB)):
        lam, gv = ssd_back_step(i, lam, gv, err, ecol, x, b, c, cum_cols, state, gmask, unit, normed, pairs, gate,
                                across, dcp, dx, dbc.at[0], dbc.at[1], sums, cross)
        value_back_step(i, p, dx, dop, dqkv)
        if i % (NB // 2) == 0:
            send_pair(i // (NB // 2)).start()
    gr = ssd_finish(aux, rate, sums, cross, gstep)
    small[...] = jnp.concatenate(
        [jnp.sum(gv, axis=0, keepdims=True), jnp.broadcast_to(gr[0:1], (1, D)), jnp.broadcast_to(gr[1:2], (1, D)),
         jnp.broadcast_to(0.5 * jnp.sum(loss, axis=1, keepdims=True), (1, D)), jnp.zeros((4, D), F32)], axis=0)
    small_x[rollout] = small[...]

    def send_x(o):
        d = lax.rem(rollout + o, 4)
        return put(small, small_x.at[rollout], s_x, d, rollout, rollout=d)

    def send_gs(d):
        return put(gstep.at[:, block(d)], gs_in.at[me], s_gs, d, me, context=d)

    def send_small(d):
        return put(small_sum, small_all.at[me], s_sm, d, me, context=d)

    def send_d(d):
        return put(dsum.at[block(d)], dall.at[me], s_d, d, me, context=d)

    def send_out(d):
        return put(dqkv.at[pl.ds(0, 2), block(d)], land.at[me, pl.ds(0, 2)], s_out, d, me, context=d)

    def send_dv(d):
        return put(dqkv.at[2, block(d)], land.at[me, 2], s_out2, d, me, context=d)

    others(me, lambda d: send_dv(d).start())
    for o in range(1, 4):
        send_x(o).start()
    q, k, v = qkv.at[0], qkv.at[1], qkv.at[2]
    for i in reversed(range(NB)):
        attention_back_step(i, q, k, v, p, x, dop, dk_acc, dqkv)
        if i == NB - 1:
            send_pair(0).wait_recv()
            send_pair(1).wait_recv()
            dsum[...] = (dbc[core].astype(F32) + dpair[...].astype(F32)).astype(BF16)
            others(me, lambda d: send_d(d).start())
            dall[me] = dsum[block(me)]
            others(me, lambda d: send_gs(d).start())
            gs_in[me] = gstep[:, block(me)]
        if i == NB - 2:
            for o in range(1, 4):
                d = lax.rem(rollout + o, 4)
                put(small, small_x.at[d], s_x, d, d, rollout=d).wait_recv()
            small_sum[...] = (small_x[0] + small_x[1]) + (small_x[2] + small_x[3])
            others(me, lambda d: send_small(d).start())
            small_all[me] = small_sum[...]
    others(me, lambda d: send_out(d).start())
    land[me] = dqkv[:, block(me)]

    others(me, lambda s: put(dsum.at[block(s)], dall.at[s], s_d, s, s, context=s).wait_recv())
    total = dall[0].astype(F32)
    for s in range(1, CTX):
        total = total + dall[s].astype(F32)
    gres[...] = total
    swap = put(gres, gother, s_g, 0, 0, head=twin)
    swap.start()
    others(me, lambda s: put(gstep.at[:, block(s)], gs_in.at[s], s_gs, s, s, context=s).wait_recv())
    rest_out[256:288, :] = jnp.concatenate([gs_in[s, 0:2] for s in range(CTX)], axis=0)
    others(me, lambda s: put(small_sum, small_all.at[s], s_sm, s, s, context=s).wait_recv())
    rest_out[288:, :] = jnp.concatenate([small_all[s] for s in range(CTX)], axis=0)
    swap.wait_recv()
    mine, other = gres[...], gother[...]
    rest_out[0:128, :] = jnp.where(core == 0, mine, other)
    rest_out[128:256, :] = jnp.where(core == 0, other, mine)
    others(me, lambda s: put(dqkv.at[2, block(s)], land.at[s, 2], s_out2, s, s, context=s).wait_recv())
    others(
        me,
        lambda s: put(dqkv.at[pl.ds(0, 2), block(s)], land.at[s, pl.ds(0, 2)], s_out, s, s, context=s).wait_recv(),
    )
    land_out[...] = land[...]

    def sent(d):
        send_qkv(d).wait_send()
        send_v(d).wait_send()
        send_aux(d).wait_send()
        send_bc(d).wait_send()
        send_twin(d).wait_send()
        put(vchip, vall.at[me], s_v, d, me, context=d).wait_send()
        send_gs(d).wait_send()
        send_d(d).wait_send()
        send_small(d).wait_send()
        send_out(d).wait_send()
        send_dv(d).wait_send()

    others(me, sent)
    for o in range(1, 4):
        send_x(o).wait_send()
    for i in range(2):
        send_pair(i).wait_send()
    pair.wait_send()
    swap.wait_send()


def place_kernel(land_in, rest_in, lengths, dqkv_out, gb_out, gc_out, gs_out, gvalue_out, grate_out, loss_out,
                 land, rest, sem):
    copies = [pltpu.make_async_copy(land_in.at[:, i], land.at[i], sem.at[i]) for i in range(3)]
    copies.append(pltpu.make_async_copy(rest_in, rest, sem.at[3]))
    for copy in copies:
        copy.start()
    copies[3].wait()
    gb_out[...] = rest[0:128, :]
    gc_out[...] = rest[128:256, :]
    gs_out[...] = rest[256:288, :]
    lane = iota((1, 32), 1)
    grate = jnp.zeros((1, 32), F32)
    for s in range(CTX):
        gvalue_out[s : s + 1, :] = rest[288 + 8 * s : 289 + 8 * s, :]
        for h in range(2):
            row = 289 + 8 * s + h
            grate = jnp.where(lane == 2 * s + h, rest[row : row + 1, 0:32], grate)
    grate_out[...] = grate
    count = lengths[0] + lengths[1] + lengths[2] + lengths[3]
    loss_out[...] = rest[291:292, 0:1] / jnp.full((1, 1), count, jnp.int32).astype(F32)
    for i in range(3):
        copies[i].wait()
        dqkv_out[i] = jnp.swapaxes(land[i], 0, 1)


def sds(shape, dtype):
    return jax.ShapeDtypeStruct(shape, dtype)


def vmem(*shape, dtype=F32):
    return pltpu.VMEM(shape, dtype)


def dma(n):
    return pltpu.SemaphoreType.DMA((2, n))


def run_heads(*args):
    whole = pl.BlockSpec(memory_space=pltpu.VMEM)
    smem = pl.BlockSpec(memory_space=pltpu.SMEM)
    plane = (T, D)
    made = pl.pallas_call(
        heads_kernel,
        out_shape=(sds((CTX, 3, TOK, D), BF16), sds((416, D), F32)),
        in_specs=[whole] * 8 + [smem],
        out_specs=[whole] * 2,
        scratch_shapes=[
            vmem(CTX, 3, TOK, D, dtype=BF16), vmem(3, T, D, dtype=BF16), vmem(2, T, D, dtype=BF16),
            vmem(CTX, 8, TOK), vmem(8, T), vmem(T, T, dtype=BF16), vmem(T, D, dtype=BF16), vmem(8, T), vmem(*plane),
            vmem(NB, D, D), vmem(2, T, W, dtype=BF16), vmem(2, T, W, dtype=BF16), vmem(2, T, W, dtype=BF16),
            vmem(*plane), vmem(*plane), vmem(*plane),
            vmem(2, T, W, dtype=BF16), vmem(T, W, dtype=BF16), vmem(8, T), vmem(*plane),
            vmem(CTX, TOK), vmem(CTX, TOK), vmem(CTX, TOK), vmem(CTX, CTX, TOK), vmem(8, T), vmem(*plane),
            vmem(*plane), vmem(*plane), vmem(T, D, dtype=BF16), vmem(3, T, D, dtype=BF16),
            vmem(2, T, D, dtype=BF16), vmem(T, D, dtype=BF16), vmem(T, D, dtype=BF16), vmem(CTX, TOK, D, dtype=BF16),
            vmem(TOK, D), vmem(TOK, D), vmem(8 * NB, W), vmem(8 * NB, W), vmem(8, T), vmem(CTX, 8, TOK),
            vmem(8, D), vmem(4, 8, D), vmem(8, D), vmem(CTX, 8, D), vmem(CTX, 3, TOK, D, dtype=BF16),
            dma(CTX), dma(CTX), dma(CTX), dma(CTX), dma(1), dma(CTX), dma(2), dma(CTX), dma(1), dma(CTX), dma(4),
            dma(CTX), dma(CTX), dma(CTX), dma(CTX),
        ],
        compiler_params=pltpu.CompilerParams(vmem_limit_bytes=60 * 2**20, collective_id=0, has_side_effects=True),
        name="heads",
    )(*args)
    return pl.pallas_call(
        place_kernel,
        out_shape=(sds((3, TOK, CTX, D), BF16), sds((TOK, D), F32), sds((TOK, D), F32), sds((32, TOK), F32),
                   sds((CTX, D), F32), sds((1, 32), F32), sds((1, 1), F32)),
        in_specs=[pl.BlockSpec(memory_space=pl.ANY)] * 2 + [smem],
        out_specs=[whole] * 7,
        scratch_shapes=[vmem(3, CTX, TOK, D, dtype=BF16), vmem(416, D), pltpu.SemaphoreType.DMA((4,))],
        name="place",
        compiler_params=pltpu.CompilerParams(vmem_limit_bytes=60 * 2**20),
    )(*made, args[-1])


def local(qkv, ssd_b, ssd_c, step_size, decay_rate, value_weight, returns, step_labels, lengths):
    dqkv, gb, gc, gs, gvalue, grate, loss = run_heads(
        qkv[:, 0], ssd_b[0], ssd_c[0], step_size[0].T, step_labels, returns, decay_rate[None],
        value_weight.reshape(CTX, D), lengths)
    return (loss.reshape(()), dqkv[:, None], gb[None], gc[None], gs.T[None], grate.reshape(-1), gvalue.reshape(-1))


def solution(mesh):
    in_specs = (
        P(None, "rollout", "context", "head", None), P("rollout", "context", None), P("rollout", "context", None),
        P("rollout", "context", "head"), P("head"), P("head"), P("rollout", None), P("rollout", "context"), P(),
    )
    out_specs = (
        P(), P(None, "rollout", "context", "head", None), P("rollout", "context", None),
        P("rollout", "context", None), P("rollout", "context", "head"), P("head"), P("head"),
    )
    return jax.shard_map(local, mesh=mesh, in_specs=in_specs, out_specs=out_specs, check_vma=False)
```

```python
import functools
import math

import jax
import jax.numpy as jnp
from jax import lax
from jax.experimental import pallas as pl
from jax.experimental.pallas import tpu as pltpu
from jax.sharding import PartitionSpec as P

NORM_EPS = 1e-05
HI = lax.Precision.HIGHEST
F32 = jnp.float32
BF16 = jnp.bfloat16
T = 2048
W = 256
NB = T // W
D = 128
SCALE = 1.0 / math.sqrt(128.0)
LOG2E = 1.4426950408889634


def dot_nn(a, b, precision=None):
    return lax.dot_general(a, b, (((1,), (0,)), ((), ())), precision=precision, preferred_element_type=F32)


def dot_nt(a, b, precision=None):
    return lax.dot_general(a, b, (((1,), (1,)), ((), ())), precision=precision, preferred_element_type=F32)


def dot_tn(a, b, precision=None):
    return lax.dot_general(a, b, (((0,), (0,)), ((), ())), precision=precision, preferred_element_type=F32)


def parts3(a):
    high = a.astype(BF16).astype(F32)
    mid = (a - high).astype(BF16).astype(F32)
    low = a - high - mid
    return jnp.concatenate([high, mid, low, jnp.zeros_like(a)], axis=0).astype(BF16)


def wide(a):
    high, low = parts(a)
    return jnp.concatenate([high, low], axis=1)


def fold(a):
    return a[:, :D] + a[:, D:]


def parts(a):
    high = a.astype(BF16)
    return high, (a - high.astype(F32)).astype(BF16)


def rows(i):
    return pl.ds(i * W, W)


def iota(shape, dim):
    return lax.broadcasted_iota(jnp.int32, shape, dim)


def head_select():
    return jnp.where(iota((8, D), 1) // 64 == iota((8, D), 0), 1.0, 0.0).astype(F32)


def head_mean():
    return jnp.where(iota((D, D), 0) // 64 == iota((D, D), 1) // 64, 1.0 / 64.0, 0.0).astype(F32)


def attention_probs(q, k, p, arrive):
    causal = iota((W, W), 0) >= iota((W, W), 1)
    c = SCALE * LOG2E
    for i in range(NB):
        arrive(i)
        qi = q[rows(i), :]
        diag = jnp.where(causal, dot_nt(qi, k[rows(i), :]) * c, -1e30)
        top = jnp.max(diag, axis=1, keepdims=True)
        if i:
            past = dot_nt(qi, k[: i * W, :]) * c
            top = jnp.maximum(top, jnp.max(past, axis=1, keepdims=True))
            past = jnp.exp2(past - top)
        diag = jnp.exp2(diag - top)
        total = jnp.sum(diag, axis=1, keepdims=True)
        if i:
            total = total + jnp.sum(past, axis=1, keepdims=True)
        inverse = 1.0 / total
        p[rows(i), rows(i)] = (diag * inverse).astype(BF16)
        if i:
            p[rows(i), : i * W] = (past * inverse).astype(BF16)


def attention_mix(p, v, x, arrive):
    for i in range(NB):
        arrive(i)
        n = (i + 1) * W
        x[rows(i), :] = dot_nn(p[rows(i), :n], v[:n, :]).astype(BF16)


def ssd_prepare(b, c, step, rate, cum_rows, cum_cols, mask, gmask, glow):
    upto = jnp.where(iota((W, W), 0) <= iota((W, W), 1), 1.0, 0.0).astype(BF16)
    causal = iota((W, W), 0) >= iota((W, W), 1)
    hsel = head_select()
    hsel4 = jnp.concatenate([hsel] * 4, axis=0).astype(BF16)
    la = jnp.concatenate([-(step[:, rows(i)] * rate) for i in range(NB)], axis=0)
    sums = dot_nn(parts3(la), upto)
    sums = sums[: 8 * NB] + sums[8 * NB : 16 * NB] + sums[16 * NB : 24 * NB]
    for i in range(NB):
        cr = sums[8 * i : 8 * i + 8]
        ce = dot_tn(parts3(cr), hsel4)
        cum_rows[:, rows(i)] = cr
        cum_cols[rows(i), :] = ce
        g = dot_nt(c[rows(i), :], b[rows(i), :])
        for h in range(2):
            gap = ce[:, 64 * h : 64 * h + 1] - cr[h : h + 1, :]
            m = jnp.exp(jnp.where(causal, gap, -1e30))
            high, low = parts(g * m)
            mask[h, rows(i), :] = m.astype(BF16)
            gmask[h, rows(i), :] = high
            glow[h, rows(i), :] = low


def ssd_forward(x, b, c, w1, cum_cols, state, gmask, glow, unit, normed, carried, value):
    hmean = head_mean().astype(BF16)
    first = iota((W, D), 1) < 64
    w8 = jnp.broadcast_to(w1, (8, D)).astype(BF16)
    st = jnp.zeros((D, D), F32)

    def mean(a):
        high, low = parts(a)
        return dot_nn(high, hmean) + dot_nn(low, hmean)

    for i in range(NB):
        ce = cum_cols[rows(i), :]
        end = ce[W - 1 : W, :]
        bi, ci, xi = b[rows(i), :], c[rows(i), :], x[rows(i), :]
        state[i] = st
        ca = jnp.exp(ce) * fold(dot_nn(ci, wide(st)))
        carried[rows(i), :] = ca
        y = ca
        for h in range(2):
            xh = jnp.where(first == (h == 0), xi, jnp.zeros_like(xi))
            y = y + dot_nn(gmask[h, rows(i), :], xh) + dot_nn(glow[h, rows(i), :], xh)
        st = jnp.exp(end) * st + fold(dot_tn(bi, wide(xi.astype(F32) * jnp.exp(end - ce))))
        r = lax.rsqrt(mean(y * y) + NORM_EPS)
        n = y * r
        unit[rows(i), :] = r * (w1 - n * mean(n * w1))
        normed[rows(i), :] = n
        high, low = parts(n)
        part = dot_nt(w8, high) + dot_nt(w8, low)
        value[2 * i : 2 * i + 1, :] = part[0:1, :D]
        value[2 * i + 1 : 2 * i + 2, :] = part[0:1, D:]


def ssd_pairs(x, b, cum_cols, state, mask, gmask, unit, carried, pairs, gate, across, dcp):
    hselb = head_select().astype(BF16)
    first = iota((W, D), 1) < 64
    for i in range(NB):
        xi, u = x[rows(i), :], unit[rows(i), :]
        dg, row = None, None
        for h in range(2):
            high, low = parts(jnp.where(first == (h == 0), u, 0.0))
            ux = dot_nt(high, xi) + dot_nt(low, xi)
            part = ux * mask[h, rows(i), :].astype(F32)
            dg = part if dg is None else dg + part
            pair = (ux * gmask[h, rows(i), :].astype(F32)).astype(BF16)
            pairs[h, rows(i), :] = pair
            pick = jnp.where(iota((8, W), 0) == h, 1.0, 0.0).astype(BF16)
            term = dot_nt(pick, pair)
            row = term if row is None else row + term
        dgb = dg.astype(BF16)
        gate[rows(i), :] = dgb
        high, low = parts(u * carried[rows(i), :])
        across[:, rows(i)] = row + dot_nt(hselb, high) + dot_nt(hselb, low)
        ue = (u * jnp.exp(cum_cols[rows(i), :])).astype(BF16)
        dcp[rows(i), :] = dot_nn(dgb, b[rows(i), :]) + dot_nt(ue, state[i].astype(BF16))


def ssd_back_step(i, lam, gv, err, ecol, x, b, c, cum_cols, state, gmask, unit, normed, pairs, gate, across, dcp,
                  dx, db, dc, sums, cross):
    hsel = head_select()
    first = iota((W, D), 1) < 64
    ce = cum_cols[rows(i), :]
    end = ce[W - 1 : W, :]
    expc, tail, decay = jnp.exp(ce), jnp.exp(end - ce), jnp.exp(end)
    bi, ci, xi = b[rows(i), :], c[rows(i), :], x[rows(i), :]
    ee, er = ecol[rows(i), :], err[:, rows(i)]
    dy = ee * unit[rows(i), :]
    bl = fold(dot_nn(bi, wide(lam)))
    xt = xi.astype(F32) * tail
    dxi = tail * bl
    col = None
    for h in range(2):
        gm = gmask[h, rows(i), :]
        dxi = dxi + fold(dot_tn(gm, wide(jnp.where(first == (h == 0), dy, 0.0))))
        eh = jnp.where(iota((8, W), 0) == h, er, 0.0)
        high = eh.astype(BF16).astype(F32)
        two = dot_nn(jnp.concatenate([high, eh - high], axis=0).astype(BF16), pairs[h, rows(i), :])
        two = two[:8] + two[8:]
        col = two if col is None else col + two
    dx[rows(i), :] = dxi
    st = state[i]
    dc[rows(i), :] = (ee * dcp[rows(i), :]).astype(BF16)
    db[rows(i), :] = (
        dot_tn(gate[rows(i), :], (ee * ci.astype(F32)).astype(BF16)) + dot_nt(xt.astype(BF16), lam.astype(BF16))
    ).astype(BF16)
    through = jnp.sum(hsel * (decay * jnp.sum(st * lam, axis=0, keepdims=True)), axis=1, keepdims=True)
    sums[8 * i : 8 * i + 8, :] = er * across[:, rows(i)] - col + jnp.where(iota((8, W), 1) == W - 1, through, 0.0)
    high, low = parts(xt * bl)
    hselb = hsel.astype(BF16)
    cross[8 * i : 8 * i + 8, :] = dot_nt(hselb, high) + dot_nt(hselb, low)
    gv = gv + jnp.sum((ee * normed[rows(i), :]).reshape(W // 8, 8, D), axis=0)
    lam = decay * lam + fold(dot_tn(ci, wide(dy * expc)))
    return lam, gv


def ssd_finish(step, rate, sums, cross, gstep):
    suffix = jnp.where(iota((W, W), 0) >= iota((W, W), 1), 1.0, 0.0).astype(BF16)
    prefix = jnp.where(iota((W, W), 0) < iota((W, W), 1), 1.0, 0.0).astype(BF16)
    g = dot_nn(parts3(sums[...]), suffix) + dot_nn(parts3(cross[...]), prefix)
    g = g[: 8 * NB] + g[8 * NB : 16 * NB] + g[16 * NB : 24 * NB]
    gr = jnp.zeros((8, W), F32)
    for i in range(NB):
        gi = g[8 * i : 8 * i + 8]
        gstep[:, rows(i)] = -(gi * rate)
        gr = gr - gi * step[:, rows(i)]
    return jnp.sum(gr, axis=1, keepdims=True)


def value_back_step(i, p, dx, dop, dqkv):
    dop[rows(i), :] = dx[rows(i), :].astype(BF16)
    dqkv[2, rows(i), :] = dot_tn(p[i * W :, rows(i)], dop[i * W :, :]).astype(BF16)


def attention_back_step(i, k, v, p, x, dop, dqkv):
    n = (i + 1) * W
    do = dop[rows(i), :]
    delta = jnp.sum(do.astype(F32) * x[rows(i), :].astype(F32), axis=1, keepdims=True)
    ds = (p[rows(i), :n].astype(F32) * (dot_nt(do, v[:n, :]) - delta)).astype(BF16)
    p[rows(i), :n] = ds
    dqkv[0, rows(i), :] = (dot_nn(ds, k[:n, :]) * SCALE).astype(BF16)


def key_back_step(j, q, p, dqkv):
    dqkv[1, rows(j), :] = (dot_tn(p[j * W :, rows(j)], q[j * W :, :]) * SCALE).astype(BF16)


MESH = pl.DeviceIdType.MESH
CTX = 16
TOK = 128


def put(src, dst, sems, slot_out, slot_in, **where):
    return pltpu.make_async_remote_copy(
        src_ref=src, dst_ref=dst, send_sem=sems.at[0, slot_out], recv_sem=sems.at[1, slot_in],
        device_id=where, device_id_type=MESH,
    )


def block(i):
    return pl.ds(pl.multiple_of(i * TOK, TOK), TOK)


def others(me, act):
    def body(o, carry):
        act(lax.rem(me + o, CTX))
        return carry

    lax.fori_loop(1, CTX, body, 0)


def heads_kernel(qkv_in, b_in, c_in, step_in, labels, table, rate_in, weight_in, lengths,
                 land_out, rest_out,
                 stage, qkv, bc, aux_out, aux, p, x, cum_rows, cum_cols, state, mask, gmask, glow, unit, normed, carried,
                 pairs, gate, across, dcp, vpart, vpair, vchip, vall, err, ecol, dx, dop, dqkv,
                 dbc, dpair, dsum, dall, gres, gother, sums, cross, gstep, gs_in, small, small_x, small_sum, small_all,
                 land, s_qkv, s_bc, s_twin, s_aux, s_vp, s_v, s_dp, s_d, s_g, s_gs, s_x, s_sm, s_out, s_qkv2, s_out2, s_out3):
    me = lax.axis_index("context")
    core = lax.axis_index("head")
    rollout = lax.axis_index("rollout")
    twin = 1 - core
    barrier = pltpu.get_barrier_semaphore()
    others(me, lambda d: pl.semaphore_signal(barrier, inc=1, device_id={"context": d}, device_id_type=MESH))
    pl.semaphore_signal(barrier, inc=1, device_id={"head": twin}, device_id_type=MESH)
    for o in range(1, 4):
        pl.semaphore_signal(barrier, inc=1, device_id={"rollout": lax.rem(rollout + o, 4)}, device_id_type=MESH)

    onehot = jnp.where(iota((64, TOK), 0) == labels[...], 1.0, 0.0).astype(F32)
    target = dot_nn(jnp.broadcast_to(table[...], (8, 64)), onehot, HI)[0:1]
    for d in range(CTX):
        aux_out[d] = jnp.concatenate([step_in[2 * d : 2 * d + 2, :], target, jnp.zeros((5, TOK), F32)], axis=0)
    bc[0, block(me)] = b_in[...]
    bc[1, block(me)] = c_in[...]
    pl.semaphore_wait(barrier, CTX + 3)

    def send_aux(d):
        return put(aux_out.at[d], aux.at[:, block(me)], s_aux, d, me, context=d)

    def send_bc(d):
        return put(bc.at[core, block(me)], bc.at[core, block(me)], s_bc, d, me, context=d)

    def send_qkv(d):
        return put(stage.at[d, pl.ds(0, 2)], qkv.at[pl.ds(0, 2), block(me)], s_qkv, d, me, context=d)

    def send_v(d):
        return put(stage.at[d, 2], qkv.at[2, block(me)], s_qkv2, d, me, context=d)

    def send_early(d):
        send_aux(d).start()

    others(me, send_early)
    for i in range(3):
        stage[:, i] = jnp.swapaxes(qkv_in[i], 0, 1)
    others(me, lambda d: send_qkv(d).start())
    others(me, lambda d: send_bc(d).start())
    others(me, lambda d: send_v(d).start())
    qkv[:, block(me)] = stage[me]
    aux[:, block(me)] = aux_out[me]
    rate = jnp.sum(
        jnp.where((iota((8, 32), 1) == 2 * me + iota((8, 32), 0)) & (iota((8, 32), 0) < 2), rate_in[...], 0.0),
        axis=1, keepdims=True,
    )
    w1 = jnp.sum(jnp.where(iota((CTX, D), 0) == me, weight_in[...].astype(F32), 0.0), axis=0, keepdims=True)

    def arrive(i):
        for s in (2 * i, 2 * i + 1):
            @pl.when(me != s)
            def _():
                put(stage.at[s, pl.ds(0, 2)], qkv.at[pl.ds(0, 2), block(s)], s_qkv, s, s, context=s).wait_recv()

    def arrive_v(i):
        for s in (2 * i, 2 * i + 1):
            @pl.when(me != s)
            def _():
                put(stage.at[s, 2], qkv.at[2, block(s)], s_qkv2, s, s, context=s).wait_recv()

    attention_probs(qkv.at[0], qkv.at[1], p, arrive)
    def got_bc(s):
        put(bc.at[core, block(s)], bc.at[core, block(s)], s_bc, s, s, context=s).wait_recv()

    others(me, got_bc)

    def send_twin(s):
        return put(bc.at[core, block(s)], bc.at[core, block(s)], s_twin, s, s, head=twin)

    others(me, lambda s: send_twin(s).start())
    others(me, lambda s: put(aux_out.at[s], aux.at[:, block(s)], s_aux, s, s, context=s).wait_recv())
    others(me, lambda s: put(bc.at[twin, block(s)], bc.at[twin, block(s)], s_twin, s, s, head=twin).wait_recv())
    b, c = bc.at[0], bc.at[1]
    ssd_prepare(b, c, aux, rate, cum_rows, cum_cols, mask, gmask, glow)
    attention_mix(p, qkv.at[2], x, arrive_v)

    ssd_forward(x, b, c, w1, cum_cols, state, gmask, glow, unit, normed, carried, vpart)

    pair = put(vpart, vpair, s_vp, 0, 0, head=twin)
    pair.start()
    pair.wait_recv()
    vchip[...] = vpart[...] + vpair[...]
    vall[me] = vchip[...]
    others(me, lambda d: put(vchip, vall.at[me], s_v, d, me, context=d).start())
    ssd_pairs(x, b, cum_cols, state, mask, gmask, unit, carried, pairs, gate, across, dcp)
    others(me, lambda s: put(vchip, vall.at[s], s_v, s, s, context=s).wait_recv())
    value = vall[0]
    for s in range(1, CTX):
        value = value + vall[s]
    limit = lengths[rollout]
    loss = jnp.zeros((1, TOK), F32)
    for s in range(CTX):
        valid = jnp.where(iota((1, TOK), 1) + s * TOK < limit, 1.0, 0.0).astype(F32)
        e = (value[s : s + 1] - aux[2:3, s * TOK : (s + 1) * TOK]) * valid
        loss = loss + e * e
        err[:, s * TOK : (s + 1) * TOK] = jnp.broadcast_to(e, (8, TOK))
    row0 = jnp.where(iota((8, D), 0) == 0, 1.0, 0.0).astype(F32)
    ecol[...] = dot_tn(parts3(err[...]), jnp.concatenate([row0] * 4, axis=0).astype(BF16))

    half = T // 2

    def send_pair(i):
        part = pl.ds(i * half, half)
        return put(dbc.at[twin, part], dpair.at[part], s_dp, i, i, head=twin)

    lam = jnp.zeros((D, D), F32)
    gv = jnp.zeros((8, D), F32)
    for i in reversed(range(NB)):
        lam, gv = ssd_back_step(i, lam, gv, err, ecol, x, b, c, cum_cols, state, gmask, unit, normed, pairs, gate,
                                across, dcp, dx, dbc.at[0], dbc.at[1], sums, cross)
        value_back_step(i, p, dx, dop, dqkv)
        if i % (NB // 2) == 0:
            send_pair(i // (NB // 2)).start()
    gr = ssd_finish(aux, rate, sums, cross, gstep)
    small[...] = jnp.concatenate(
        [jnp.sum(gv, axis=0, keepdims=True), jnp.broadcast_to(gr[0:1], (1, D)), jnp.broadcast_to(gr[1:2], (1, D)),
         jnp.broadcast_to(0.5 * jnp.sum(loss, axis=1, keepdims=True), (1, D)), jnp.zeros((4, D), F32)], axis=0)
    small_x[rollout] = small[...]

    def send_x(o):
        d = lax.rem(rollout + o, 4)
        return put(small, small_x.at[rollout], s_x, d, rollout, rollout=d)

    def send_gs(d):
        return put(gstep.at[:, block(d)], gs_in.at[me], s_gs, d, me, context=d)

    def send_small(d):
        return put(small_sum, small_all.at[me], s_sm, d, me, context=d)

    def send_d(d):
        return put(dsum.at[block(d)], dall.at[me], s_d, d, me, context=d)

    def send_out(d):
        return put(dqkv.at[0, block(d)], land.at[me, 0], s_out, d, me, context=d)

    def send_dk(d):
        return put(dqkv.at[1, block(d)], land.at[me, 1], s_out3, d, me, context=d)

    def send_dv(d):
        return put(dqkv.at[2, block(d)], land.at[me, 2], s_out2, d, me, context=d)

    others(me, lambda d: send_dv(d).start())
    for o in range(1, 4):
        send_x(o).start()
    q, k, v = qkv.at[0], qkv.at[1], qkv.at[2]
    for i in reversed(range(NB)):
        attention_back_step(i, k, v, p, x, dop, dqkv)
        if i == NB - 1:
            send_pair(0).wait_recv()
            send_pair(1).wait_recv()
            dsum[...] = (dbc[core].astype(F32) + dpair[...].astype(F32)).astype(BF16)
            others(me, lambda d: send_d(d).start())
            dall[me] = dsum[block(me)]
            others(me, lambda d: send_gs(d).start())
            gs_in[me] = gstep[:, block(me)]
        if i == NB - 2:
            for o in range(1, 4):
                d = lax.rem(rollout + o, 4)
                put(small, small_x.at[d], s_x, d, d, rollout=d).wait_recv()
            small_sum[...] = (small_x[0] + small_x[1]) + (small_x[2] + small_x[3])
            others(me, lambda d: send_small(d).start())
            small_all[me] = small_sum[...]
    others(me, lambda d: send_out(d).start())
    for j in range(NB):
        key_back_step(j, q, p, dqkv)
    others(me, lambda d: send_dk(d).start())
    land[me] = dqkv[:, block(me)]

    others(me, lambda s: put(dsum.at[block(s)], dall.at[s], s_d, s, s, context=s).wait_recv())
    total = dall[0].astype(F32)
    for s in range(1, CTX):
        total = total + dall[s].astype(F32)
    gres[...] = total
    swap = put(gres, gother, s_g, 0, 0, head=twin)
    swap.start()
    others(me, lambda s: put(gstep.at[:, block(s)], gs_in.at[s], s_gs, s, s, context=s).wait_recv())
    rest_out[256:288, :] = jnp.concatenate([gs_in[s, 0:2] for s in range(CTX)], axis=0)
    others(me, lambda s: put(small_sum, small_all.at[s], s_sm, s, s, context=s).wait_recv())
    rest_out[288:, :] = jnp.concatenate([small_all[s] for s in range(CTX)], axis=0)
    swap.wait_recv()
    mine, other = gres[...], gother[...]
    rest_out[0:128, :] = jnp.where(core == 0, mine, other)
    rest_out[128:256, :] = jnp.where(core == 0, other, mine)
    others(me, lambda s: put(dqkv.at[2, block(s)], land.at[s, 2], s_out2, s, s, context=s).wait_recv())
    others(me, lambda s: put(dqkv.at[0, block(s)], land.at[s, 0], s_out, s, s, context=s).wait_recv())
    others(me, lambda s: put(dqkv.at[1, block(s)], land.at[s, 1], s_out3, s, s, context=s).wait_recv())
    land_out[...] = land[...]

    def sent(d):
        send_qkv(d).wait_send()
        send_v(d).wait_send()
        send_aux(d).wait_send()
        send_bc(d).wait_send()
        send_twin(d).wait_send()
        put(vchip, vall.at[me], s_v, d, me, context=d).wait_send()
        send_gs(d).wait_send()
        send_d(d).wait_send()
        send_small(d).wait_send()
        send_out(d).wait_send()
        send_dv(d).wait_send()
        send_dk(d).wait_send()

    others(me, sent)
    for o in range(1, 4):
        send_x(o).wait_send()
    for i in range(2):
        send_pair(i).wait_send()
    pair.wait_send()
    swap.wait_send()


def place_kernel(land_in, rest_in, lengths, dqkv_out, gb_out, gc_out, gs_out, gvalue_out, grate_out, loss_out,
                 land, rest, sem):
    copies = [pltpu.make_async_copy(land_in.at[:, i], land.at[i], sem.at[i]) for i in range(3)]
    copies.append(pltpu.make_async_copy(rest_in, rest, sem.at[3]))
    for copy in copies:
        copy.start()
    copies[3].wait()
    gb_out[...] = rest[0:128, :]
    gc_out[...] = rest[128:256, :]
    gs_out[...] = rest[256:288, :]
    lane = iota((1, 32), 1)
    grate = jnp.zeros((1, 32), F32)
    for s in range(CTX):
        gvalue_out[s : s + 1, :] = rest[288 + 8 * s : 289 + 8 * s, :]
        for h in range(2):
            row = 289 + 8 * s + h
            grate = jnp.where(lane == 2 * s + h, rest[row : row + 1, 0:32], grate)
    grate_out[...] = grate
    count = lengths[0] + lengths[1] + lengths[2] + lengths[3]
    loss_out[...] = rest[291:292, 0:1] / jnp.full((1, 1), count, jnp.int32).astype(F32)
    for i in range(3):
        copies[i].wait()
        dqkv_out[i] = jnp.swapaxes(land[i], 0, 1)


def sds(shape, dtype):
    return jax.ShapeDtypeStruct(shape, dtype)


def vmem(*shape, dtype=F32):
    return pltpu.VMEM(shape, dtype)


def dma(n):
    return pltpu.SemaphoreType.DMA((2, n))


def run_heads(*args):
    whole = pl.BlockSpec(memory_space=pltpu.VMEM)
    smem = pl.BlockSpec(memory_space=pltpu.SMEM)
    plane = (T, D)
    made = pl.pallas_call(
        heads_kernel,
        out_shape=(sds((CTX, 3, TOK, D), BF16), sds((416, D), F32)),
        in_specs=[whole] * 8 + [smem],
        out_specs=[whole] * 2,
        scratch_shapes=[
            vmem(CTX, 3, TOK, D, dtype=BF16), vmem(3, T, D, dtype=BF16), vmem(2, T, D, dtype=BF16),
            vmem(CTX, 8, TOK), vmem(8, T), vmem(T, T, dtype=BF16), vmem(T, D, dtype=BF16), vmem(8, T), vmem(*plane),
            vmem(NB, D, D), vmem(2, T, W, dtype=BF16), vmem(2, T, W, dtype=BF16), vmem(2, T, W, dtype=BF16),
            vmem(*plane), vmem(*plane), vmem(*plane),
            vmem(2, T, W, dtype=BF16), vmem(T, W, dtype=BF16), vmem(8, T), vmem(*plane),
            vmem(CTX, TOK), vmem(CTX, TOK), vmem(CTX, TOK), vmem(CTX, CTX, TOK), vmem(8, T), vmem(*plane),
            vmem(*plane), vmem(T, D, dtype=BF16), vmem(3, T, D, dtype=BF16),
            vmem(2, T, D, dtype=BF16), vmem(T, D, dtype=BF16), vmem(T, D, dtype=BF16), vmem(CTX, TOK, D, dtype=BF16),
            vmem(TOK, D), vmem(TOK, D), vmem(8 * NB, W), vmem(8 * NB, W), vmem(8, T), vmem(CTX, 8, TOK),
            vmem(8, D), vmem(4, 8, D), vmem(8, D), vmem(CTX, 8, D), vmem(CTX, 3, TOK, D, dtype=BF16),
            dma(CTX), dma(CTX), dma(CTX), dma(CTX), dma(1), dma(CTX), dma(2), dma(CTX), dma(1), dma(CTX), dma(4),
            dma(CTX), dma(CTX), dma(CTX), dma(CTX), dma(CTX),
        ],
        compiler_params=pltpu.CompilerParams(vmem_limit_bytes=60 * 2**20, collective_id=0, has_side_effects=True),
        name="heads",
    )(*args)
    return pl.pallas_call(
        place_kernel,
        out_shape=(sds((3, TOK, CTX, D), BF16), sds((TOK, D), F32), sds((TOK, D), F32), sds((32, TOK), F32),
                   sds((CTX, D), F32), sds((1, 32), F32), sds((1, 1), F32)),
        in_specs=[pl.BlockSpec(memory_space=pl.ANY)] * 2 + [smem],
        out_specs=[whole] * 7,
        scratch_shapes=[vmem(3, CTX, TOK, D, dtype=BF16), vmem(416, D), pltpu.SemaphoreType.DMA((4,))],
        name="place",
        compiler_params=pltpu.CompilerParams(vmem_limit_bytes=60 * 2**20),
    )(*made, args[-1])


def local(qkv, ssd_b, ssd_c, step_size, decay_rate, value_weight, returns, step_labels, lengths):
    dqkv, gb, gc, gs, gvalue, grate, loss = run_heads(
        qkv[:, 0], ssd_b[0], ssd_c[0], step_size[0].T, step_labels, returns, decay_rate[None],
        value_weight.reshape(CTX, D), lengths)
    return (loss.reshape(()), dqkv[:, None], gb[None], gc[None], gs.T[None], grate.reshape(-1), gvalue.reshape(-1))


def solution(mesh):
    in_specs = (
        P(None, "rollout", "context", "head", None), P("rollout", "context", None), P("rollout", "context", None),
        P("rollout", "context", "head"), P("head"), P("head"), P("rollout", None), P("rollout", "context"), P(),
    )
    out_specs = (
        P(), P(None, "rollout", "context", "head", None), P("rollout", "context", None),
        P("rollout", "context", None), P("rollout", "context", "head"), P("head"), P("head"),
    )
    return jax.shard_map(local, mesh=mesh, in_specs=in_specs, out_specs=out_specs, check_vma=False)
```
